512 devices in a mesh: depth: 32 (over x, y, core), strip: 16 (over z).
Axes of the slice: x: 4, y: 4, z: 16, core: 2. Of those that a mesh axis runs over, the one named last changes fastest.
Arguments:
- density: float32 [128, 256, 2048], P('depth', 'strip'), may hold values from -6 to 6
- materials: int32 [128, 256, 2048], P('depth', 'strip'), may hold values from 0 to 3
- occupancy_flags: int32 [32, 16, 16], P('depth', 'strip'), may hold values from 0 to 1, as said below
- tf_color: float32 [4, 3, 16], replicated, may hold values from 0.1 to 1
- tf_opacity: float32 [4, 16], replicated, may hold values from 0.0005 to 0.05
Outputs:
- image: float32 [4, 256, 2048], P(None, 'strip', 'depth')
The draws below stay inside these ranges and needn't reach their ends.
Inputs may be any that keep to these rules, and one draw needn't show every extreme that they name: `occupancy_flags`: occupied tiles cluster around one depth slab drawn from the seed; the share of occupied tiles differs strongly between depth slabs.
All inputs are finite; a program needn't handle non-finite values.
Results may differ from the reference program's by a relative error of at most 0.0003.
Values sent between devices are 32-bit elements; how exact they have to be, the bound alone decides.
A program may use at most 64 MiB of HBM per device.

```python
import math
import jax
import jax.numpy as jnp
from jax import lax

DZ = 4
RY = 16
COLS = 2048
KNOTS = 16
MATS = 4
TILES = 16
NZ = 128
NY = 256
N_DEPTH = 32
N_STRIP = 16


def draw_occupancy_flags(key, part):
    key_centre = jax.random.fold_in(key, 11)
    key_rolls = jax.random.fold_in(key, 23)
    centre = jax.random.randint(key_centre, (), 0, N_DEPTH)
    depth_pos = jnp.arange(N_DEPTH, dtype=jnp.int32)[:, None, None]
    distance = jnp.abs(depth_pos - centre)
    chance = jnp.maximum(15, 95 - 160 * distance // N_DEPTH)
    dice_rolls = jax.random.randint(key_rolls, (N_DEPTH, N_STRIP, TILES), 0, 100)
    return (dice_rolls < chance).astype(jnp.int32)


def touch_ends(values, rng, low, top_value):
    longest = values.shape.index(max(values.shape))
    spots = []
    for shift in (0, 1):
        where = [jax.random.randint(jax.random.fold_in(rng, axis), (), 0, length) for axis, length in enumerate(values.shape)]
        where[longest] = (where[longest] + shift) % values.shape[longest]
        spots.append(tuple(where))
    return values.at[spots[0]].set(low).at[spots[1]].set(top_value)


def block_scale(rng, extent, split, least, largest):
    def one(dim, parts):
        draws = jax.random.uniform(jax.random.fold_in(jax.random.fold_in(rng, 6), dim), (parts,), jnp.float32, least / len(split), largest / len(split))
        return jnp.repeat(jnp.exp(draws), extent[dim] // parts).reshape((-1,) + (1,) * (len(extent) - dim - 1))

    loudness = one(*split[0])
    for cut in split[1:]:
        loudness = loudness * one(*cut)
    return loudness


def centred(key, dims, spread, limit, split=(), held_as=jnp.bfloat16):
    values = jax.random.normal(key, dims, jnp.float32) * spread
    if len(split) > 0:
        values = block_scale(key, dims, split, -0.22, 0.18) * values
    return jnp.clip(values, min=-limit, max=limit).astype(held_as)


def setup_inputs(seed: int = 0) -> dict:
    seeds = jax.random.split(jax.random.key(seed), 6)
    density = centred(seeds[0], (NZ, NY, COLS), 1.0, 6.0, ((0, 32), (1, 16)), jnp.float32)
    materials = touch_ends(jax.random.randint(seeds[1], (NZ, NY, COLS), 0, MATS), jax.random.fold_in(seeds[1], 1), 0, MATS - 1).astype(jnp.int32)
    occupancy_flags = draw_occupancy_flags(jax.random.fold_in(seeds[5], 71), 0)
    tf_color = jnp.clip(jax.random.uniform(seeds[3], (MATS, 3, KNOTS), jnp.float32, 0.1, 1.0), 0.1, 1.0)
    tf_opacity = jnp.clip(jnp.exp(jax.random.uniform(seeds[4], (MATS, KNOTS), jnp.float32, math.log(0.0005), math.log(0.05))), 0.0005, 0.05)
    return dict(density=density, materials=materials, occupancy_flags=occupancy_flags, tf_color=tf_color, tf_opacity=tf_opacity)


light_x = 1.0 / 3.0
light_y = 2.0 / 3.0
light_z = 2.0 / 3.0
ambient = 0.3
diffuse = 0.7

def shade_slice(before, here, after, material_slice, occupied, knot_table):
    sample = here[1:-1, 1:-1]
    grad_z = 0.5 * (after[1:-1, 1:-1] - before[1:-1, 1:-1])
    grad_y = 0.5 * (here[2:, 1:-1] - here[:-2, 1:-1])
    grad_x = 0.5 * (here[1:-1, 2:] - here[1:-1, :-2])
    knot_count = knot_table.shape[1]
    material_count = knot_table.shape[0] // 4
    position = jnp.clip((sample.reshape(-1) + 3.0) * ((knot_count - 1) / 6.0), 0.0, knot_count - 1.0)
    knot_grid = jnp.arange(knot_count, dtype=jnp.float32)[:, None]
    tent_weights = jnp.maximum(0.0, 1.0 - jnp.abs(position[None, :] - knot_grid))
    looked = jnp.dot(knot_table, tent_weights, precision=lax.Precision.HIGHEST, preferred_element_type=jnp.float32)
    onehot = (material_slice.reshape(-1)[None, :] == jnp.arange(material_count, dtype=jnp.int32)[:, None]).astype(jnp.float32)
    colour = lax.optimization_barrier(jnp.sum(looked[:3 * material_count].reshape(material_count, 3, -1) * onehot[:, None, :], axis=0))
    density_rate = lax.optimization_barrier(jnp.sum(looked[3 * material_count:] * onehot, axis=0)) * occupied.reshape(-1)
    facing = (grad_x * light_x + grad_y * light_y + grad_z * light_z).reshape(-1)
    steepness = (grad_x * grad_x + grad_y * grad_y + grad_z * grad_z).reshape(-1)
    lighting = ambient + diffuse * jnp.abs(facing) / jnp.sqrt(1.0 + steepness)
    opacity_step = 1.0 - jnp.exp(-density_rate)
    return (colour * (lighting * opacity_step)[None, :], opacity_step)

def reference(density, materials, occupancy_flags, tf_color, tf_opacity):
    knot_table = jnp.concatenate([tf_color.reshape(MATS * 3, KNOTS), tf_opacity], axis=0)
    padded = jnp.pad(density, 1)

    def advance(state_carry, slab_index):
        radiance, transmit = state_carry
        before = lax.dynamic_index_in_dim(padded, slab_index, 0, keepdims=False)
        here = lax.dynamic_index_in_dim(padded, slab_index + 1, 0, keepdims=False)
        after = lax.dynamic_index_in_dim(padded, slab_index + 2, 0, keepdims=False)
        material_slice = lax.dynamic_index_in_dim(materials, slab_index, 0, keepdims=False)
        tile_flags = lax.dynamic_index_in_dim(occupancy_flags, slab_index // DZ, 0, keepdims=False)
        occupied = jnp.repeat(jnp.repeat(tile_flags, RY, axis=0), COLS // TILES, axis=1).astype(jnp.float32)
        emitted, opacity_step = shade_slice(before, here, after, material_slice, occupied, knot_table)
        return ((radiance + transmit[None, :] * emitted, transmit * (1.0 - opacity_step)), None)
    start = (jnp.zeros((3, NY * COLS), jnp.float32), jnp.ones((NY * COLS,), jnp.float32))
    (radiance, transmit), _ = lax.scan(advance, start, jnp.arange(NZ, dtype=jnp.int32))
    return jnp.concatenate([radiance.reshape(3, NY, COLS), (1.0 - transmit).reshape(1, NY, COLS)], axis=0)
```

```python
import jax
import jax.numpy as jnp
from jax import lax
from jax.experimental import pallas as pl
from jax.experimental.pallas import tpu as pltpu
from jax.sharding import PartitionSpec as P

MESH = pl.DeviceIdType.MESH
LANES = 128
HALF = LANES // 2
SIDE = 4
CHIPS = SIDE * SIDE
ORDER = (2, 1, 3, 0)


def kernel(
    density, materials, flags, tf_color, tf_opacity, image,
    field, mats, top, bottom, shade, through, packed, outgoing, pieces,
    load_sem, plane_send, plane_recv, row_send, row_recv,
    core_send, core_recv, piece_send, piece_recv,
):
    depth_count = lax.axis_size("depth")
    strip_count = lax.axis_size("strip")
    d = lax.axis_index("depth")
    s = lax.axis_index("strip")
    core = lax.rem(d, 2)
    chip = d // 2
    chip_x = chip // SIDE
    partner = d + 1 - 2 * core
    cross = d - 1 + 2 * core
    cross_ok = jnp.logical_and(cross >= 0, cross < depth_count)
    planes, rows, columns = density.shape
    chunk = columns // SIDE
    tiles = columns // LANES
    per_chunk = chunk // LANES

    barrier = pltpu.get_barrier_semaphore()

    def greet(**where):
        pl.semaphore_signal(barrier, inc=1, device_id=where, device_id_type=MESH)

    greet(depth=partner)
    pl.when(cross_ok)(lambda: greet(depth=cross))
    pl.when(s > 0)(lambda: greet(strip=s - 1))
    pl.when(s < strip_count - 1)(lambda: greet(strip=s + 1))

    @pl.loop(0, CHIPS)
    def _(k):
        pl.when(k != chip)(lambda: greet(depth=2 * k + core))

    def load(j):
        cols = pl.ds(j * chunk, chunk)
        return (
            pltpu.make_async_copy(
                density.at[:, :, cols],
                field.at[pl.ds(1, planes), :, pl.ds(j * chunk + LANES, chunk)],
                load_sem.at[0, j],
            ),
            pltpu.make_async_copy(
                materials.at[:, :, cols], mats.at[:, :, cols], load_sem.at[1, j]
            ),
        )

    for j in range(SIDE):
        for copy in load(j):
            copy.start()

    edge = jnp.zeros((planes, rows, LANES), jnp.float32)
    field[pl.ds(1, planes), :, pl.ds(0, LANES)] = edge
    field[pl.ds(1, planes), :, pl.ds(columns + LANES, LANES)] = edge

    expected = (
        CHIPS
        + cross_ok.astype(jnp.int32)
        + (s > 0).astype(jnp.int32)
        + (s < strip_count - 1).astype(jnp.int32)
    )
    pl.semaphore_wait(barrier, expected)

    def plane_copy(way, j):
        j = pl.multiple_of(j * chunk, LANES)
        source = planes - 1 if way == 0 else 0
        target = 0 if way == 0 else planes + 1
        at = j // chunk
        return pltpu.make_async_remote_copy(
            src_ref=density.at[source, :, pl.ds(j, chunk)],
            dst_ref=field.at[target, :, pl.ds(j + LANES, chunk)],
            send_sem=plane_send.at[way, at],
            recv_sem=plane_recv.at[way, at],
            device_id={"depth": d + 1 if way == 0 else d - 1},
            device_id_type=MESH,
        )

    def row_copy(way):
        source = rows - 1 if way == 0 else 0
        return pltpu.make_async_remote_copy(
            src_ref=density.at[:, pl.ds(source, 1), :],
            dst_ref=top if way == 0 else bottom,
            send_sem=row_send.at[way],
            recv_sem=row_recv.at[way],
            device_id={"strip": s + 1 if way == 0 else s - 1},
            device_id_type=MESH,
        )

    has_next = d < depth_count - 1
    has_before = d > 0
    has_below = s < strip_count - 1
    has_above = s > 0

    def owner(j):
        return lax.rem(chip_x + ORDER[j], SIDE)

    pl.when(has_below)(lambda: row_copy(0).start())
    pl.when(has_above)(lambda: row_copy(1).start())
    for j in range(SIDE):
        pl.when(has_next)(lambda: plane_copy(0, owner(j)).start())
        pl.when(has_before)(lambda: plane_copy(1, owner(j)).start())

    @pl.when(jnp.logical_not(has_before))
    def _():
        field[0] = jnp.zeros(field.shape[1:], jnp.float32)

    @pl.when(jnp.logical_not(has_next))
    def _():
        field[planes + 1] = jnp.zeros(field.shape[1:], jnp.float32)

    @pl.when(jnp.logical_not(has_above))
    def _():
        top[...] = jnp.zeros(top.shape, jnp.float32)

    @pl.when(jnp.logical_not(has_below))
    def _():
        bottom[...] = jnp.zeros(bottom.shape, jnp.float32)

    material_count, _, knots = tf_color.shape
    lane = lax.broadcasted_iota(jnp.int32, (8, LANES), 1)
    sub = lax.broadcasted_iota(jnp.int32, (8, LANES), 0)

    def table(row_of):
        parts = [row_of(m) for m in range(material_count)]
        parts.append(jnp.zeros((1, LANES - material_count * knots), jnp.float32))
        base = jnp.broadcast_to(jnp.concatenate(parts, axis=1), (8, LANES))
        return base, pltpu.roll(base, LANES - 1, 1) - base

    tables = [table(lambda m, c=c: tf_color[m, pl.ds(c, 1), :]) for c in range(3)]
    tables.append(table(lambda m: tf_opacity[pl.ds(m, 1), :]))

    def look(entry, index):
        return jnp.take_along_axis(entry, index, axis=1, mode="promise_in_bounds")

    for j in range(SIDE):
        for copy in load(j):
            copy.wait()

        @pl.loop(j * per_chunk, (j + 1) * per_chunk)
        def _(t):
            at = pl.multiple_of(t * LANES, LANES)
            occupied = flags[0, 0, t].astype(jnp.float32)
            for half in range(rows // 8):
                band = pl.ds(8 * half, 8)
                passed = jnp.ones((8, LANES), jnp.float32)
                for z in range(planes):
                    sample = field[z + 1, band, pl.ds(at + LANES, LANES)]
                    position = jnp.clip((sample + 3.0) * ((knots - 1) / 6.0), 0.0, knots - 1.0)
                    knot = position.astype(jnp.int32)
                    part = position - knot.astype(jnp.float32)
                    index = (mats[z, band, pl.ds(at, LANES)] * knots + knot) & (LANES - 1)
                    values = [look(b, index) + part * look(g, index) for b, g in tables]
                    kept = jnp.exp(-(values[3] * occupied))
                    weight = passed * (1.0 - kept)
                    for c in range(3):
                        shade[c, z, band, pl.ds(at, LANES)] = values[c] * weight
                    passed = passed * kept
                through[band, pl.ds(at, LANES)] = passed

    pl.when(has_above)(lambda: row_copy(0).wait_recv())
    pl.when(has_below)(lambda: row_copy(1).wait_recv())

    def core_copy(j):
        mine = pl.ds(j * per_chunk, per_chunk)
        return pltpu.make_async_remote_copy(
            src_ref=packed.at[1 - core, mine],
            dst_ref=packed.at[2, mine],
            send_sem=core_send.at[j],
            recv_sem=core_recv.at[j],
            device_id={"depth": partner},
            device_id_type=MESH,
        )

    def piece_copy(k, source):
        return pltpu.make_async_remote_copy(
            src_ref=outgoing.at[k],
            dst_ref=pieces.at[source],
            send_sem=piece_send.at[k],
            recv_sem=piece_recv.at[source],
            device_id={"depth": 2 * k + core},
            device_id_type=MESH,
        )

    def light_tile(t):
        at = pl.multiple_of(t * LANES, LANES)

        def tile(z, half, shift=0):
            return field[z, pl.ds(8 * half, 8), pl.ds(at + LANES + shift * LANES, LANES)]

        sums = [[None] * 4 for _ in range(2)]
        for half in range(2):
            sums[half][3] = through[pl.ds(8 * half, 8), pl.ds(at, LANES)]
        column = [[tile(z, half) for half in range(2)] for z in range(planes + 2)]
        for z in range(planes):
            above = jnp.broadcast_to(top[z, :, pl.ds(at, LANES)], (8, LANES))
            below = jnp.broadcast_to(bottom[z, :, pl.ds(at, LANES)], (8, LANES))
            here = column[z + 1]
            for half in range(2):
                mid = here[half]
                left = pltpu.roll(jnp.where(lane == LANES - 1, tile(z + 1, half, -1), mid), 1, 1)
                right = pltpu.roll(jnp.where(lane == 0, tile(z + 1, half, 1), mid), LANES - 1, 1)
                up = pltpu.roll(jnp.where(sub == 7, above if half == 0 else here[0], mid), 1, 0)
                down = pltpu.roll(jnp.where(sub == 0, below if half == 1 else here[1], mid), 7, 0)
                gx = right - left
                gy = down - up
                gz = column[z + 2][half] - column[z][half]
                facing = gx + 2.0 * (gy + gz)
                steep = gx * gx + gy * gy + gz * gz
                light = 0.3 + (0.7 / 3.0) * jnp.abs(facing) * lax.rsqrt(4.0 + steep)
                for c in range(3):
                    term = shade[c, z, pl.ds(8 * half, 8), pl.ds(at, LANES)] * light
                    sums[half][c] = term if z == 0 else sums[half][c] + term
        return sums

    def pack(j):
        @pl.loop(0, per_chunk)
        def _(y):
            sums = light_tile(owner(j) * per_chunk + y)
            for c in range(4):
                first, second = sums[0][c], sums[1][c]
                packed[0, j * per_chunk + y, c] = jnp.where(
                    lane < HALF, first, pltpu.roll(second, HALF, 1)
                )
                packed[1, j * per_chunk + y, c] = jnp.where(
                    lane < HALF, pltpu.roll(first, HALF, 1), second
                )

    def join(j):
        core_copy(j).wait_recv()

        @pl.loop(0, per_chunk)
        def _(y):
            k = owner(j) * SIDE + y
            near = packed.at[2 * core, j * per_chunk + y]
            far = packed.at[2 - core, j * per_chunk + y]
            passed = near[3]
            for c in range(3):
                outgoing[k, c] = near[c] + passed * far[c]
            outgoing[k, 3] = passed * far[3]

        @pl.loop(0, per_chunk)
        def _(y):
            k = owner(j) * SIDE + y
            pl.when(k != chip)(lambda: piece_copy(k, chip).start())

    for j in range(SIDE):
        pl.when(has_before)(lambda: plane_copy(0, owner(j)).wait_recv())
        pl.when(has_next)(lambda: plane_copy(1, owner(j)).wait_recv())
        pack(j)
        core_copy(j).start()
        if j > 0:
            join(j - 1)
    join(SIDE - 1)

    pieces[chip] = outgoing[chip]

    @pl.loop(0, CHIPS)
    def _(k):
        pl.when(k != chip)(lambda: piece_copy(k, k).wait_recv())

    def over(k, held):
        passed = held[3]
        return tuple(held[c] + passed * pieces[k, c] for c in range(3)) + (
            passed * pieces[k, 3],
        )

    start = tuple(pieces[0, c] for c in range(4))
    held = lax.fori_loop(1, CHIPS, over, start)
    for c in range(4):
        value = held[c] if c < 3 else 1.0 - held[c]
        image[c, pl.ds(0, 8), :] = value[:, :HALF]
        image[c, pl.ds(8, 8), :] = pltpu.roll(value, HALF, 1)[:, :HALF]

    pl.when(has_below)(lambda: row_copy(0).wait_send())
    pl.when(has_above)(lambda: row_copy(1).wait_send())
    for j in range(SIDE):
        pl.when(has_next)(lambda: plane_copy(0, owner(j)).wait_send())
        pl.when(has_before)(lambda: plane_copy(1, owner(j)).wait_send())
        core_copy(j).wait_send()

    @pl.loop(0, CHIPS)
    def _(k):
        pl.when(k != chip)(lambda: piece_copy(k, chip).wait_send())


def on_device(density, materials, occupancy_flags, tf_color, tf_opacity):
    planes, rows, columns = density.shape
    tiles = columns // LANES
    block = (4, 8, LANES)
    f32 = jnp.float32
    dma = pltpu.SemaphoreType.DMA
    return pl.pallas_call(
        kernel,
        out_shape=jax.ShapeDtypeStruct((4, rows, columns // lax.axis_size("depth")), f32),
        in_specs=[
            pl.BlockSpec(memory_space=pltpu.HBM),
            pl.BlockSpec(memory_space=pltpu.HBM),
            pl.BlockSpec(memory_space=pltpu.SMEM),
            pl.BlockSpec(memory_space=pltpu.VMEM),
            pl.BlockSpec(memory_space=pltpu.VMEM),
        ],
        out_specs=pl.BlockSpec(memory_space=pltpu.VMEM),
        scratch_shapes=[
            pltpu.VMEM((planes + 2, rows, columns + 2 * LANES), f32),
            pltpu.VMEM((planes, rows, columns), jnp.int32),
            pltpu.VMEM((planes, 1, columns), f32),
            pltpu.VMEM((planes, 1, columns), f32),
            pltpu.VMEM((3, planes, rows, columns), f32),
            pltpu.VMEM((rows, columns), f32),
            pltpu.VMEM((3, tiles) + block, f32),
            pltpu.VMEM((CHIPS,) + block, f32),
            pltpu.VMEM((CHIPS,) + block, f32),
            dma((2, SIDE)),
            dma((2, SIDE)),
            dma((2, SIDE)),
            dma((2,)),
            dma((2,)),
            dma((SIDE,)),
            dma((SIDE,)),
            dma((CHIPS,)),
            dma((CHIPS,)),
        ],
        compiler_params=pltpu.CompilerParams(
            collective_id=0, has_side_effects=True, vmem_limit_bytes=60 << 20
        ),
        name="render",
    )(density, materials, occupancy_flags, tf_color, tf_opacity)


def solution(mesh):
    placed = (
        P("depth", "strip", None),
        P("depth", "strip", None),
        P("depth", "strip", None),
        P(),
        P(),
    )
    return jax.shard_map(
        on_device, mesh=mesh, in_specs=placed, out_specs=P(None, "strip", "depth"), check_vma=False
    )
```

```python
import jax
import jax.numpy as jnp
from jax import lax
from jax.experimental import pallas as pl
from jax.experimental.pallas import tpu as pltpu
from jax.sharding import PartitionSpec as P

MESH = pl.DeviceIdType.MESH
LANES = 128
HALF = LANES // 2
SIDE = 4
CHIPS = SIDE * SIDE
LOOK_UNROLL = 4
LIGHT_UNROLL = 2
ORDER = (2, 1, 3, 0)


def kernel(
    density, materials, flags_in, color_in, opacity_in, image,
    field, mats, top, bottom, shade, through, packed, outgoing, pieces,
    looked, flags, tf_color, tf_opacity, small_sem, relay,
    load_sem, plane_send, plane_recv, row_send, row_recv,
    core_send, core_recv, piece_send, piece_recv,
):
    depth_count = lax.axis_size("depth")
    strip_count = lax.axis_size("strip")
    d = lax.axis_index("depth")
    s = lax.axis_index("strip")
    core = lax.rem(d, 2)
    chip = d // 2
    chip_x = chip // SIDE
    partner = d + 1 - 2 * core
    cross = d - 1 + 2 * core
    cross_ok = jnp.logical_and(cross >= 0, cross < depth_count)
    planes, rows, columns = density.shape
    chunk = columns // SIDE
    tiles = columns // LANES
    per_chunk = chunk // LANES

    chip_y = lax.rem(chip, SIDE)

    def on_chip(x, y):
        return 2 * (lax.rem(x, SIDE) * SIDE + lax.rem(y, SIDE)) + core

    along_x = [on_chip(chip_x + step, chip_y) for step in (1, SIDE - 1)]
    along_y = [on_chip(chip_x, chip_y + step) for step in (1, SIDE - 1)]
    barrier = pltpu.get_barrier_semaphore()

    def tell(sem, **where):
        pl.semaphore_signal(sem, inc=1, device_id=where, device_id_type=MESH)

    pl.when(cross_ok)(lambda: tell(barrier, depth=cross))
    pl.when(s > 0)(lambda: tell(barrier, strip=s - 1))
    pl.when(s < strip_count - 1)(lambda: tell(barrier, strip=s + 1))
    tell(barrier, depth=partner)
    for other in along_x + along_y:
        tell(barrier, depth=other)

    def load(j):
        start = pl.multiple_of(j * chunk, LANES)
        cols = pl.ds(start, chunk)
        return (
            pltpu.make_async_copy(
                density.at[:, :, cols],
                field.at[pl.ds(1, planes), :, pl.ds(start + LANES, chunk)],
                load_sem.at[0, j],
            ),
            pltpu.make_async_copy(
                materials.at[:, :, cols], mats.at[:, :, cols], load_sem.at[1, j]
            ),
        )

    small = (
        pltpu.make_async_copy(flags_in, flags, small_sem.at[0]),
        pltpu.make_async_copy(color_in, tf_color, small_sem.at[1]),
        pltpu.make_async_copy(opacity_in, tf_opacity, small_sem.at[2]),
    )
    for copy in small:
        copy.start()
    for j in range(SIDE):
        for copy in load(j):
            copy.start()

    edge = jnp.zeros((planes, rows, LANES), jnp.float32)
    field[pl.ds(1, planes), :, pl.ds(0, LANES)] = edge
    field[pl.ds(1, planes), :, pl.ds(columns + LANES, LANES)] = edge

    expected = (
        1
        + len(along_x)
        + len(along_y)
        + cross_ok.astype(jnp.int32)
        + (s > 0).astype(jnp.int32)
        + (s < strip_count - 1).astype(jnp.int32)
    )
    pl.semaphore_wait(barrier, expected)

    def plane_copy(way, j):
        j = pl.multiple_of(j * chunk, LANES)
        source = planes - 1 if way == 0 else 0
        target = 0 if way == 0 else planes + 1
        at = j // chunk
        return pltpu.make_async_remote_copy(
            src_ref=density.at[source, :, pl.ds(j, chunk)],
            dst_ref=field.at[target, :, pl.ds(j + LANES, chunk)],
            send_sem=plane_send.at[way, at],
            recv_sem=plane_recv.at[way, at],
            device_id={"depth": d + 1 if way == 0 else d - 1},
            device_id_type=MESH,
        )

    def row_copy(way):
        source = rows - 1 if way == 0 else 0
        return pltpu.make_async_remote_copy(
            src_ref=density.at[:, pl.ds(source, 1), :],
            dst_ref=top if way == 0 else bottom,
            send_sem=row_send.at[way],
            recv_sem=row_recv.at[way],
            device_id={"strip": s + 1 if way == 0 else s - 1},
            device_id_type=MESH,
        )

    has_next = d < depth_count - 1
    has_before = d > 0
    has_below = s < strip_count - 1
    has_above = s > 0

    def owner(j):
        return lax.rem(chip_x + ORDER[j], SIDE)

    pl.when(has_below)(lambda: row_copy(0).start())
    pl.when(has_above)(lambda: row_copy(1).start())
    for j in range(SIDE):
        pl.when(has_next)(lambda: plane_copy(0, owner(j)).start())
        pl.when(has_before)(lambda: plane_copy(1, owner(j)).start())

    def relay_on(step, others):
        for other in others:
            tell(relay.at[step], depth=other)

    def relayed(step):
        pl.semaphore_wait(relay.at[step], 2)

    relay_on(0, along_y)

    @pl.when(jnp.logical_not(has_before))
    def _():
        field[0] = jnp.zeros(field.shape[1:], jnp.float32)

    @pl.when(jnp.logical_not(has_next))
    def _():
        field[planes + 1] = jnp.zeros(field.shape[1:], jnp.float32)

    @pl.when(jnp.logical_not(has_above))
    def _():
        top[...] = jnp.zeros(top.shape, jnp.float32)

    @pl.when(jnp.logical_not(has_below))
    def _():
        bottom[...] = jnp.zeros(bottom.shape, jnp.float32)

    _, material_count, knots = tf_color.shape
    for copy in small:
        copy.wait()
    lane = lax.broadcasted_iota(jnp.int32, (8, LANES), 1)
    sub = lax.broadcasted_iota(jnp.int32, (8, LANES), 0)

    def table(row_of):
        parts = [row_of(m) for m in range(material_count)]
        parts.append(jnp.zeros((1, LANES - material_count * knots), jnp.float32))
        base = jnp.broadcast_to(jnp.concatenate(parts, axis=1), (8, LANES))
        return base, pltpu.roll(base, LANES - 1, 1) - base

    tables = [table(lambda m, c=c: tf_color[c, pl.ds(m, 1), :]) for c in range(3)]
    tables.append(table(lambda m: tf_opacity[pl.ds(m, 1), :]))

    along_lanes = lax.GatherDimensionNumbers(
        offset_dims=(),
        collapsed_slice_dims=(1,),
        start_index_map=(1,),
        operand_batching_dims=(0,),
        start_indices_batching_dims=(0,),
    )

    def look(entry, index):
        return lax.gather(
            entry,
            index[:, :, None],
            along_lanes,
            slice_sizes=(1, 1),
            mode=lax.GatherScatterMode.PROMISE_IN_BOUNDS,
        )

    cells = [(z, half) for half in range(rows // 8) for z in range(planes)]

    def look_up_tile(t, slot):
        at = pl.multiple_of(t * LANES, LANES)
        for n, (z, half) in enumerate(cells):
            band = pl.ds(8 * half, 8)
            sample = field[z + 1, band, pl.ds(at + LANES, LANES)]
            position = jnp.clip((sample + 3.0) * ((knots - 1) / 6.0), 0.0, knots - 1.0)
            knot = position.astype(jnp.int32)
            part = position - knot.astype(jnp.float32)
            index = (mats[z, band, pl.ds(at, LANES)] * knots + knot) & (LANES - 1)
            for c, (base, step) in enumerate(tables):
                looked[slot, n, c] = look(base, index) + part * look(step, index)

    def weigh_tile(t, slot):
        at = pl.multiple_of(t * LANES, LANES)
        occupied = flags[0, 0, t].astype(jnp.float32)
        passed = None
        for n, (z, half) in enumerate(cells):
            band = pl.ds(8 * half, 8)
            kept = jnp.exp(-(looked[slot, n, 3] * occupied))
            weight = 1.0 - kept if z == 0 else passed * (1.0 - kept)
            for c in range(3):
                shade[c, z, band, pl.ds(at, LANES)] = looked[slot, n, c] * weight
            passed = kept if z == 0 else passed * kept
            if z == planes - 1:
                through[band, pl.ds(at, LANES)] = passed

    def look_up(i):
        for u in range(LOOK_UNROLL):
            look_up_tile(i * LOOK_UNROLL + u, u)

    def weigh(i):
        for u in range(LOOK_UNROLL):
            weigh_tile(i * LOOK_UNROLL + u, u)

    def loaded(j):
        for copy in load(j):
            copy.wait()

    steps = per_chunk // LOOK_UNROLL

    def weigh_and_look_up(i):
        weigh(i - 1)
        look_up(i)

    loaded(0)
    look_up(0)
    pl.loop(1, steps)(weigh_and_look_up)
    relayed(0)
    relay_on(1, along_x)

    @pl.loop(1, SIDE)
    def _(j):
        loaded(j)
        pl.loop(j * steps, (j + 1) * steps)(weigh_and_look_up)

    relayed(1)
    relay_on(2, along_x)
    weigh(SIDE * steps - 1)

    pl.when(has_above)(lambda: row_copy(0).wait_recv())
    pl.when(has_below)(lambda: row_copy(1).wait_recv())

    def core_copy(j):
        mine = pl.ds(j * per_chunk, per_chunk)
        return pltpu.make_async_remote_copy(
            src_ref=packed.at[1 - core, mine],
            dst_ref=packed.at[2, mine],
            send_sem=core_send.at[j],
            recv_sem=core_recv.at[j],
            device_id={"depth": partner},
            device_id_type=MESH,
        )

    def piece_copy(k, source):
        return pltpu.make_async_remote_copy(
            src_ref=outgoing.at[k],
            dst_ref=pieces.at[source],
            send_sem=piece_send.at[k],
            recv_sem=piece_recv.at[source],
            device_id={"depth": 2 * k + core},
            device_id_type=MESH,
        )

    def light_tile(t):
        at = pl.multiple_of(t * LANES, LANES)

        def tile(z, half, shift=0):
            return field[z, pl.ds(8 * half, 8), pl.ds(at + LANES + shift * LANES, LANES)]

        sums = [[None] * 4 for _ in range(2)]
        for half in range(2):
            sums[half][3] = through[pl.ds(8 * half, 8), pl.ds(at, LANES)]
        column = [[tile(z, half) for half in range(2)] for z in range(planes + 2)]
        for z in range(planes):
            above = jnp.broadcast_to(top[z, :, pl.ds(at, LANES)], (8, LANES))
            below = jnp.broadcast_to(bottom[z, :, pl.ds(at, LANES)], (8, LANES))
            here = column[z + 1]
            for half in range(2):
                mid = here[half]
                left = pltpu.roll(jnp.where(lane == LANES - 1, tile(z + 1, half, -1), mid), 1, 1)
                right = pltpu.roll(jnp.where(lane == 0, tile(z + 1, half, 1), mid), LANES - 1, 1)
                up = pltpu.roll(jnp.where(sub == 7, above if half == 0 else here[0], mid), 1, 0)
                down = pltpu.roll(jnp.where(sub == 0, below if half == 1 else here[1], mid), 7, 0)
                gx = right - left
                gy = down - up
                gz = column[z + 2][half] - column[z][half]
                facing = gx + 2.0 * (gy + gz)
                steep = gx * gx + gy * gy + gz * gz
                light = 0.3 + (0.7 / 3.0) * jnp.abs(facing) * lax.rsqrt(4.0 + steep)
                for c in range(3):
                    term = shade[c, z, pl.ds(8 * half, 8), pl.ds(at, LANES)] * light
                    sums[half][c] = term if z == 0 else sums[half][c] + term
        return sums

    def pack(j):
        def pack_tile(y):
            sums = light_tile(owner(j) * per_chunk + y)
            for c in range(4):
                first, second = sums[0][c], sums[1][c]
                packed[0, j * per_chunk + y, c] = jnp.where(
                    lane < HALF, first, pltpu.roll(second, HALF, 1)
                )
                packed[1, j * per_chunk + y, c] = jnp.where(
                    lane < HALF, pltpu.roll(first, HALF, 1), second
                )

        @pl.loop(0, per_chunk // LIGHT_UNROLL)
        def _(i):
            for u in range(LIGHT_UNROLL):
                pack_tile(i * LIGHT_UNROLL + u)

    def join(j):
        if j == 0:
            relayed(2)
        core_copy(j).wait_recv()

        @pl.loop(0, per_chunk)
        def _(y):
            k = owner(j) * SIDE + y
            near = packed.at[2 * core, j * per_chunk + y]
            far = packed.at[2 - core, j * per_chunk + y]
            passed = near[3]
            for c in range(3):
                outgoing[k, c] = near[c] + passed * far[c]
            outgoing[k, 3] = passed * far[3]

        @pl.loop(0, per_chunk)
        def _(y):
            k = owner(j) * SIDE + y
            pl.when(k != chip)(lambda: piece_copy(k, chip).start())

    for j in range(SIDE):
        pl.when(has_before)(lambda: plane_copy(0, owner(j)).wait_recv())
        pl.when(has_next)(lambda: plane_copy(1, owner(j)).wait_recv())
        pack(j)
        core_copy(j).start()
        if j > 0:
            join(j - 1)
    join(SIDE - 1)

    pieces[chip] = outgoing[chip]

    @pl.loop(0, CHIPS)
    def _(k):
        pl.when(k != chip)(lambda: piece_copy(k, k).wait_recv())

    def over(k, held):
        passed = held[3]
        return tuple(held[c] + passed * pieces[k, c] for c in range(3)) + (
            passed * pieces[k, 3],
        )

    start = tuple(pieces[0, c] for c in range(4))
    held = lax.fori_loop(1, CHIPS, over, start)
    for c in range(4):
        value = held[c] if c < 3 else 1.0 - held[c]
        image[c, pl.ds(0, 8), :] = value[:, :HALF]
        image[c, pl.ds(8, 8), :] = pltpu.roll(value, HALF, 1)[:, :HALF]

    pl.when(has_below)(lambda: row_copy(0).wait_send())
    pl.when(has_above)(lambda: row_copy(1).wait_send())
    for j in range(SIDE):
        pl.when(has_next)(lambda: plane_copy(0, owner(j)).wait_send())
        pl.when(has_before)(lambda: plane_copy(1, owner(j)).wait_send())
        core_copy(j).wait_send()

    @pl.loop(0, CHIPS)
    def _(k):
        pl.when(k != chip)(lambda: piece_copy(k, chip).wait_send())


def on_device(density, materials, occupancy_flags, tf_color, tf_opacity):
    planes, rows, columns = density.shape
    tiles = columns // LANES
    color = jnp.transpose(tf_color, (1, 0, 2))
    block = (4, 8, LANES)
    f32 = jnp.float32
    dma = pltpu.SemaphoreType.DMA
    return pl.pallas_call(
        kernel,
        out_shape=jax.ShapeDtypeStruct((4, rows, columns // lax.axis_size("depth")), f32),
        in_specs=[
            pl.BlockSpec(memory_space=pltpu.HBM),
        ]
        * 5,
        out_specs=pl.BlockSpec(memory_space=pltpu.VMEM),
        scratch_shapes=[
            pltpu.VMEM((planes + 2, rows, columns + 2 * LANES), f32),
            pltpu.VMEM((planes, rows, columns), jnp.int32),
            pltpu.VMEM((planes, 1, columns), f32),
            pltpu.VMEM((planes, 1, columns), f32),
            pltpu.VMEM((3, planes, rows, columns), f32),
            pltpu.VMEM((rows, columns), f32),
            pltpu.VMEM((3, tiles) + block, f32),
            pltpu.VMEM((CHIPS,) + block, f32),
            pltpu.VMEM((CHIPS,) + block, f32),
            pltpu.VMEM((LOOK_UNROLL, 2 * planes, 4, 8, LANES), f32),
            pltpu.SMEM(occupancy_flags.shape, jnp.int32),
            pltpu.VMEM(color.shape, f32),
            pltpu.VMEM(tf_opacity.shape, f32),
            dma((3,)),
            pltpu.SemaphoreType.REGULAR((3,)),
            dma((2, SIDE)),
            dma((2, SIDE)),
            dma((2, SIDE)),
            dma((2,)),
            dma((2,)),
            dma((SIDE,)),
            dma((SIDE,)),
            dma((CHIPS,)),
            dma((CHIPS,)),
        ],
        compiler_params=pltpu.CompilerParams(
            collective_id=0, has_side_effects=True, vmem_limit_bytes=60 << 20
        ),
        name="render",
    )(density, materials, occupancy_flags, color, tf_opacity)


def solution(mesh):
    placed = (
        P("depth", "strip", None),
        P("depth", "strip", None),
        P("depth", "strip", None),
        P(),
        P(),
    )
    return jax.shard_map(
        on_device, mesh=mesh, in_specs=placed, out_specs=P(None, "strip", "depth"), check_vma=False
    )
```

```python
import jax
import jax.numpy as jnp
from jax import lax
from jax.experimental import pallas as pl
from jax.experimental.pallas import tpu as pltpu
from jax.sharding import PartitionSpec as P

MESH = pl.DeviceIdType.MESH
LANES = 128
HALF = LANES // 2
SIDE = 4
CHIPS = SIDE * SIDE
LOOK_UNROLL = 4
LIGHT_UNROLL = 2
ORDER = (2, 1, 3, 0)


def kernel(
    density, materials, flags_in, color_in, opacity_in, image,
    field, mats, top, bottom, shade, through, packed, outgoing, pieces,
    looked, flags, tf_color, tf_opacity, small_sem, relay,
    load_sem, plane_send, plane_recv, row_send, row_recv,
    core_send, core_recv, piece_send, piece_recv,
):
    depth_count = lax.axis_size("depth")
    strip_count = lax.axis_size("strip")
    d = lax.axis_index("depth")
    s = lax.axis_index("strip")
    core = lax.rem(d, 2)
    chip = d // 2
    chip_x = chip // SIDE
    partner = d + 1 - 2 * core
    cross = d - 1 + 2 * core
    cross_ok = jnp.logical_and(cross >= 0, cross < depth_count)
    planes, rows, columns = density.shape
    chunk = columns // SIDE
    tiles = columns // LANES
    per_chunk = chunk // LANES

    chip_y = lax.rem(chip, SIDE)

    def on_chip(x, y):
        return 2 * (lax.rem(x, SIDE) * SIDE + lax.rem(y, SIDE)) + core

    along_x = [on_chip(chip_x + step, chip_y) for step in (1, SIDE - 1)]
    across_x = along_x + [on_chip(chip_x + 2, chip_y)]
    along_y = [on_chip(chip_x, chip_y + step) for step in (1, SIDE - 1)]
    barrier = pltpu.get_barrier_semaphore()

    def tell(sem, **where):
        pl.semaphore_signal(sem, inc=1, device_id=where, device_id_type=MESH)

    pl.when(cross_ok)(lambda: tell(barrier, depth=cross))
    pl.when(s > 0)(lambda: tell(barrier, strip=s - 1))
    pl.when(s < strip_count - 1)(lambda: tell(barrier, strip=s + 1))
    tell(barrier, depth=partner)
    for other in along_x + along_y:
        tell(barrier, depth=other)

    def load(j):
        start = pl.multiple_of(j * chunk, LANES)
        cols = pl.ds(start, chunk)
        return (
            pltpu.make_async_copy(
                density.at[:, :, cols],
                field.at[pl.ds(1, planes), :, pl.ds(start + LANES, chunk)],
                load_sem.at[0, j],
            ),
            pltpu.make_async_copy(
                materials.at[:, :, cols], mats.at[:, :, cols], load_sem.at[1, j]
            ),
        )

    small = (
        pltpu.make_async_copy(flags_in, flags, small_sem.at[0]),
        pltpu.make_async_copy(color_in, tf_color, small_sem.at[1]),
        pltpu.make_async_copy(opacity_in, tf_opacity, small_sem.at[2]),
    )
    for copy in small:
        copy.start()
    for j in range(SIDE):
        for copy in load(j):
            copy.start()

    edge = jnp.zeros((planes, rows, LANES), jnp.float32)
    field[pl.ds(1, planes), :, pl.ds(0, LANES)] = edge
    field[pl.ds(1, planes), :, pl.ds(columns + LANES, LANES)] = edge

    expected = (
        1
        + len(along_x)
        + len(along_y)
        + cross_ok.astype(jnp.int32)
        + (s > 0).astype(jnp.int32)
        + (s < strip_count - 1).astype(jnp.int32)
    )
    pl.semaphore_wait(barrier, expected)

    def plane_copy(way, j):
        j = pl.multiple_of(j * chunk, LANES)
        source = planes - 1 if way == 0 else 0
        target = 0 if way == 0 else planes + 1
        at = j // chunk
        return pltpu.make_async_remote_copy(
            src_ref=density.at[source, :, pl.ds(j, chunk)],
            dst_ref=field.at[target, :, pl.ds(j + LANES, chunk)],
            send_sem=plane_send.at[way, at],
            recv_sem=plane_recv.at[way, at],
            device_id={"depth": d + 1 if way == 0 else d - 1},
            device_id_type=MESH,
        )

    def row_copy(way):
        source = rows - 1 if way == 0 else 0
        return pltpu.make_async_remote_copy(
            src_ref=density.at[:, pl.ds(source, 1), :],
            dst_ref=top if way == 0 else bottom,
            send_sem=row_send.at[way],
            recv_sem=row_recv.at[way],
            device_id={"strip": s + 1 if way == 0 else s - 1},
            device_id_type=MESH,
        )

    has_next = d < depth_count - 1
    has_before = d > 0
    has_below = s < strip_count - 1
    has_above = s > 0

    def owner(j):
        return lax.rem(chip_x + ORDER[j], SIDE)

    pl.when(has_below)(lambda: row_copy(0).start())
    pl.when(has_above)(lambda: row_copy(1).start())
    for j in range(SIDE):
        pl.when(has_next)(lambda: plane_copy(0, owner(j)).start())
        pl.when(has_before)(lambda: plane_copy(1, owner(j)).start())

    def relay_on(step, others):
        for other in others:
            tell(relay.at[step], depth=other)

    def relayed(step, count):
        pl.semaphore_wait(relay.at[step], count)

    relay_on(0, along_y + along_x)

    @pl.when(jnp.logical_not(has_before))
    def _():
        field[0] = jnp.zeros(field.shape[1:], jnp.float32)

    @pl.when(jnp.logical_not(has_next))
    def _():
        field[planes + 1] = jnp.zeros(field.shape[1:], jnp.float32)

    @pl.when(jnp.logical_not(has_above))
    def _():
        top[...] = jnp.zeros(top.shape, jnp.float32)

    @pl.when(jnp.logical_not(has_below))
    def _():
        bottom[...] = jnp.zeros(bottom.shape, jnp.float32)

    _, material_count, knots = tf_color.shape
    for copy in small:
        copy.wait()
    lane = lax.broadcasted_iota(jnp.int32, (8, LANES), 1)
    sub = lax.broadcasted_iota(jnp.int32, (8, LANES), 0)

    def table(row_of):
        parts = [row_of(m) for m in range(material_count)]
        parts.append(jnp.zeros((1, LANES - material_count * knots), jnp.float32))
        base = jnp.broadcast_to(jnp.concatenate(parts, axis=1), (8, LANES))
        return base, pltpu.roll(base, LANES - 1, 1) - base

    tables = [table(lambda m, c=c: tf_color[c, pl.ds(m, 1), :]) for c in range(3)]
    tables.append(table(lambda m: tf_opacity[pl.ds(m, 1), :]))

    along_lanes = lax.GatherDimensionNumbers(
        offset_dims=(),
        collapsed_slice_dims=(1,),
        start_index_map=(1,),
        operand_batching_dims=(0,),
        start_indices_batching_dims=(0,),
    )

    def look(entry, index):
        return lax.gather(
            entry,
            index[:, :, None],
            along_lanes,
            slice_sizes=(1, 1),
            mode=lax.GatherScatterMode.PROMISE_IN_BOUNDS,
        )

    cells = [(z, half) for half in range(rows // 8) for z in range(planes)]

    def look_up_tile(t, slot):
        at = pl.multiple_of(t * LANES, LANES)
        for n, (z, half) in enumerate(cells):
            band = pl.ds(8 * half, 8)
            sample = field[z + 1, band, pl.ds(at + LANES, LANES)]
            position = jnp.clip((sample + 3.0) * ((knots - 1) / 6.0), 0.0, knots - 1.0)
            knot = position.astype(jnp.int32)
            part = position - knot.astype(jnp.float32)
            index = (mats[z, band, pl.ds(at, LANES)] * knots + knot) & (LANES - 1)
            for c, (base, step) in enumerate(tables):
                looked[slot, n, c] = look(base, index) + part * look(step, index)

    def weigh_tile(t, slot):
        at = pl.multiple_of(t * LANES, LANES)
        occupied = flags[0, 0, t].astype(jnp.float32)
        passed = None
        for n, (z, half) in enumerate(cells):
            band = pl.ds(8 * half, 8)
            kept = jnp.exp(-(looked[slot, n, 3] * occupied))
            weight = 1.0 - kept if z == 0 else passed * (1.0 - kept)
            for c in range(3):
                shade[c, z, band, pl.ds(at, LANES)] = looked[slot, n, c] * weight
            passed = kept if z == 0 else passed * kept
            if z == planes - 1:
                through[band, pl.ds(at, LANES)] = passed

    def look_up(i):
        for u in range(LOOK_UNROLL):
            look_up_tile(i * LOOK_UNROLL + u, u)

    def weigh(i):
        for u in range(LOOK_UNROLL):
            weigh_tile(i * LOOK_UNROLL + u, u)

    def loaded(j):
        for copy in load(j):
            copy.wait()

    steps = per_chunk // LOOK_UNROLL

    def weigh_and_look_up(i):
        weigh(i - 1)
        look_up(i)

    loaded(0)
    look_up(0)
    pl.loop(1, steps)(weigh_and_look_up)
    relayed(0, len(along_y + along_x))
    relay_on(1, across_x)

    @pl.loop(1, SIDE)
    def _(j):
        loaded(j)
        pl.loop(j * steps, (j + 1) * steps)(weigh_and_look_up)

    weigh(SIDE * steps - 1)

    pl.when(has_above)(lambda: row_copy(0).wait_recv())
    pl.when(has_below)(lambda: row_copy(1).wait_recv())

    def core_copy(j):
        mine = pl.ds(j * per_chunk, per_chunk)
        return pltpu.make_async_remote_copy(
            src_ref=packed.at[1 - core, mine],
            dst_ref=packed.at[2, mine],
            send_sem=core_send.at[j],
            recv_sem=core_recv.at[j],
            device_id={"depth": partner},
            device_id_type=MESH,
        )

    def piece_copy(k, source):
        return pltpu.make_async_remote_copy(
            src_ref=outgoing.at[k],
            dst_ref=pieces.at[source],
            send_sem=piece_send.at[k],
            recv_sem=piece_recv.at[source],
            device_id={"depth": 2 * k + core},
            device_id_type=MESH,
        )

    def light_tile(t):
        at = pl.multiple_of(t * LANES, LANES)

        def tile(z, half, shift=0):
            return field[z, pl.ds(8 * half, 8), pl.ds(at + LANES + shift * LANES, LANES)]

        sums = [[None] * 4 for _ in range(2)]
        for half in range(2):
            sums[half][3] = through[pl.ds(8 * half, 8), pl.ds(at, LANES)]
        column = [[tile(z, half) for half in range(2)] for z in range(planes + 2)]
        for z in range(planes):
            above = jnp.broadcast_to(top[z, :, pl.ds(at, LANES)], (8, LANES))
            below = jnp.broadcast_to(bottom[z, :, pl.ds(at, LANES)], (8, LANES))
            here = column[z + 1]
            for half in range(2):
                mid = here[half]
                left = pltpu.roll(jnp.where(lane == LANES - 1, tile(z + 1, half, -1), mid), 1, 1)
                right = pltpu.roll(jnp.where(lane == 0, tile(z + 1, half, 1), mid), LANES - 1, 1)
                up = pltpu.roll(jnp.where(sub == 7, above if half == 0 else here[0], mid), 1, 0)
                down = pltpu.roll(jnp.where(sub == 0, below if half == 1 else here[1], mid), 7, 0)
                gx = right - left
                gy = down - up
                gz = column[z + 2][half] - column[z][half]
                facing = gx + 2.0 * (gy + gz)
                steep = gx * gx + gy * gy + gz * gz
                light = 0.3 + (0.7 / 3.0) * jnp.abs(facing) * lax.rsqrt(4.0 + steep)
                for c in range(3):
                    term = shade[c, z, pl.ds(8 * half, 8), pl.ds(at, LANES)] * light
                    sums[half][c] = term if z == 0 else sums[half][c] + term
        return sums

    def pack(j):
        def pack_tile(y):
            sums = light_tile(owner(j) * per_chunk + y)
            for c in range(4):
                first, second = sums[0][c], sums[1][c]
                packed[0, j * per_chunk + y, c] = jnp.where(
                    lane < HALF, first, pltpu.roll(second, HALF, 1)
                )
                packed[1, j * per_chunk + y, c] = jnp.where(
                    lane < HALF, pltpu.roll(first, HALF, 1), second
                )

        @pl.loop(0, per_chunk // LIGHT_UNROLL)
        def _(i):
            for u in range(LIGHT_UNROLL):
                pack_tile(i * LIGHT_UNROLL + u)

    def over(near, far):
        return [near[c] + near[3] * far[c] for c in range(3)] + [near[3] * far[3]]

    def join(j):
        if j == 0:
            relayed(1, len(across_x))
        core_copy(j).wait_recv()
        for y in range(per_chunk):
            k = owner(j) * SIDE + y
            near = [packed[2 * core, j * per_chunk + y, c] for c in range(4)]
            far = [packed[2 - core, j * per_chunk + y, c] for c in range(4)]
            for c, value in enumerate(over(near, far)):
                outgoing[k, c] = value
        for y in range(per_chunk):
            k = owner(j) * SIDE + y
            pl.when(k != chip)(lambda k=k: piece_copy(k, chip).start())

    for j in range(SIDE):
        pl.when(has_before)(lambda: plane_copy(0, owner(j)).wait_recv())
        pl.when(has_next)(lambda: plane_copy(1, owner(j)).wait_recv())
        pack(j)
        core_copy(j).start()
        if j > 0:
            join(j - 1)
    join(SIDE - 1)

    pieces[chip] = outgoing[chip]

    @pl.loop(0, CHIPS)
    def _(k):
        pl.when(k != chip)(lambda: piece_copy(k, k).wait_recv())

    held = [[pieces[k, c] for c in range(4)] for k in range(CHIPS)]
    while len(held) > 1:
        held = [over(near, far) for near, far in zip(held[0::2], held[1::2])]
    held = held[0]
    for c in range(4):
        value = held[c] if c < 3 else 1.0 - held[c]
        image[c, pl.ds(0, 8), :] = value[:, :HALF]
        image[c, pl.ds(8, 8), :] = pltpu.roll(value, HALF, 1)[:, :HALF]

    pl.when(has_below)(lambda: row_copy(0).wait_send())
    pl.when(has_above)(lambda: row_copy(1).wait_send())
    for j in range(SIDE):
        pl.when(has_next)(lambda: plane_copy(0, owner(j)).wait_send())
        pl.when(has_before)(lambda: plane_copy(1, owner(j)).wait_send())
        core_copy(j).wait_send()

    @pl.loop(0, CHIPS)
    def _(k):
        pl.when(k != chip)(lambda: piece_copy(k, chip).wait_send())


def on_device(density, materials, occupancy_flags, tf_color, tf_opacity):
    planes, rows, columns = density.shape
    tiles = columns // LANES
    color = jnp.transpose(tf_color, (1, 0, 2))
    block = (4, 8, LANES)
    f32 = jnp.float32
    dma = pltpu.SemaphoreType.DMA
    return pl.pallas_call(
        kernel,
        out_shape=pltpu.VMEM((4, rows, columns // lax.axis_size("depth")), f32),
        in_specs=[
            pl.BlockSpec(memory_space=pltpu.HBM),
        ]
        * 5,
        out_specs=pl.BlockSpec(memory_space=pltpu.VMEM),
        scratch_shapes=[
            pltpu.VMEM((planes + 2, rows, columns + 2 * LANES), f32),
            pltpu.VMEM((planes, rows, columns), jnp.int32),
            pltpu.VMEM((planes, 1, columns), f32),
            pltpu.VMEM((planes, 1, columns), f32),
            pltpu.VMEM((3, planes, rows, columns), f32),
            pltpu.VMEM((rows, columns), f32),
            pltpu.VMEM((3, tiles) + block, f32),
            pltpu.VMEM((CHIPS,) + block, f32),
            pltpu.VMEM((CHIPS,) + block, f32),
            pltpu.VMEM((LOOK_UNROLL, 2 * planes, 4, 8, LANES), f32),
            pltpu.SMEM(occupancy_flags.shape, jnp.int32),
            pltpu.VMEM(color.shape, f32),
            pltpu.VMEM(tf_opacity.shape, f32),
            dma((3,)),
            pltpu.SemaphoreType.REGULAR((2,)),
            dma((2, SIDE)),
            dma((2, SIDE)),
            dma((2, SIDE)),
            dma((2,)),
            dma((2,)),
            dma((SIDE,)),
            dma((SIDE,)),
            dma((CHIPS,)),
            dma((CHIPS,)),
        ],
        compiler_params=pltpu.CompilerParams(
            collective_id=0, has_side_effects=True, vmem_limit_bytes=60 << 20
        ),
        name="render",
    )(density, materials, occupancy_flags, color, tf_opacity)


def solution(mesh):
    placed = (
        P("depth", "strip", None),
        P("depth", "strip", None),
        P("depth", "strip", None),
        P(),
        P(),
    )
    return jax.shard_map(
        on_device, mesh=mesh, in_specs=placed, out_specs=P(None, "strip", "depth"), check_vma=False
    )
```

```python
import jax
import jax.numpy as jnp
from jax import lax
from jax.experimental import pallas as pl
from jax.experimental.pallas import tpu as pltpu
from jax.sharding import PartitionSpec as P

MESH = pl.DeviceIdType.MESH
LANES = 128
HALF = LANES // 2
SIDE = 4
CHIPS = SIDE * SIDE
LOOK_UNROLL = 4
LIGHT_UNROLL = 2
ORDER = (2, 0, 1, 3)


def kernel(
    density, materials, flags_in, color_in, opacity_in, image,
    field, mats, top, bottom, shade, through, packed, outgoing, pieces,
    looked, flags, tf_color, tf_opacity, small_sem, relay,
    load_sem, plane_send, plane_recv, row_send, row_recv,
    core_send, core_recv, piece_send, piece_recv,
):
    depth_count = lax.axis_size("depth")
    strip_count = lax.axis_size("strip")
    d = lax.axis_index("depth")
    s = lax.axis_index("strip")
    core = lax.rem(d, 2)
    chip = d // 2
    chip_x = chip // SIDE
    partner = d + 1 - 2 * core
    cross = d - 1 + 2 * core
    cross_ok = jnp.logical_and(cross >= 0, cross < depth_count)
    planes, rows, columns = density.shape
    chunk = columns // SIDE
    tiles = columns // LANES
    per_chunk = chunk // LANES

    chip_y = lax.rem(chip, SIDE)

    def on_chip(x, y):
        return 2 * (lax.rem(x, SIDE) * SIDE + lax.rem(y, SIDE)) + core

    along_x = [on_chip(chip_x + step, chip_y) for step in (1, SIDE - 1)]
    across_x = along_x + [on_chip(chip_x + 2, chip_y)]
    along_y = [on_chip(chip_x, chip_y + step) for step in (1, SIDE - 1)]
    barrier = pltpu.get_barrier_semaphore()

    def tell(sem, **where):
        pl.semaphore_signal(sem, inc=1, device_id=where, device_id_type=MESH)

    pl.when(cross_ok)(lambda: tell(barrier, depth=cross))
    pl.when(s > 0)(lambda: tell(barrier, strip=s - 1))
    pl.when(s < strip_count - 1)(lambda: tell(barrier, strip=s + 1))
    tell(barrier, depth=partner)
    for other in along_x + along_y:
        tell(barrier, depth=other)

    def load(j):
        start = pl.multiple_of(j * chunk, LANES)
        cols = pl.ds(start, chunk)
        return (
            pltpu.make_async_copy(
                density.at[:, :, cols],
                field.at[pl.ds(1, planes), :, pl.ds(start + LANES, chunk)],
                load_sem.at[0, j],
            ),
            pltpu.make_async_copy(
                materials.at[:, :, cols], mats.at[:, :, cols], load_sem.at[1, j]
            ),
        )

    small = (
        pltpu.make_async_copy(flags_in, flags, small_sem.at[0]),
        pltpu.make_async_copy(color_in, tf_color, small_sem.at[1]),
        pltpu.make_async_copy(opacity_in, tf_opacity, small_sem.at[2]),
    )
    for copy in small:
        copy.start()
    for j in range(SIDE):
        for copy in load(j):
            copy.start()

    edge = jnp.zeros((planes, rows, LANES), jnp.float32)
    field[pl.ds(1, planes), :, pl.ds(0, LANES)] = edge
    field[pl.ds(1, planes), :, pl.ds(columns + LANES, LANES)] = edge

    expected = (
        1
        + len(along_x)
        + len(along_y)
        + cross_ok.astype(jnp.int32)
        + (s > 0).astype(jnp.int32)
        + (s < strip_count - 1).astype(jnp.int32)
    )
    pl.semaphore_wait(barrier, expected)

    def wanted(way, j):
        there = (d + 1 if way == 0 else d - 1) // 2 // SIDE
        return lax.rem(there + ORDER[j], SIDE)

    def plane_copy(way, j):
        j = pl.multiple_of(j * chunk, LANES)
        source = planes - 1 if way == 0 else 0
        target = 0 if way == 0 else planes + 1
        at = j // chunk
        return pltpu.make_async_remote_copy(
            src_ref=density.at[source, :, pl.ds(j, chunk)],
            dst_ref=field.at[target, :, pl.ds(j + LANES, chunk)],
            send_sem=plane_send.at[way, at],
            recv_sem=plane_recv.at[way, at],
            device_id={"depth": d + 1 if way == 0 else d - 1},
            device_id_type=MESH,
        )

    def row_copy(way):
        source = rows - 1 if way == 0 else 0
        return pltpu.make_async_remote_copy(
            src_ref=density.at[:, pl.ds(source, 1), :],
            dst_ref=top if way == 0 else bottom,
            send_sem=row_send.at[way],
            recv_sem=row_recv.at[way],
            device_id={"strip": s + 1 if way == 0 else s - 1},
            device_id_type=MESH,
        )

    has_next = d < depth_count - 1
    has_before = d > 0
    has_below = s < strip_count - 1
    has_above = s > 0

    def owner(j):
        return lax.rem(chip_x + ORDER[j], SIDE)

    pl.when(has_below)(lambda: row_copy(0).start())
    pl.when(has_above)(lambda: row_copy(1).start())
    for j in range(SIDE):
        pl.when(has_next)(lambda: plane_copy(0, wanted(0, j)).start())
        pl.when(has_before)(lambda: plane_copy(1, wanted(1, j)).start())

    def relay_on(step, others):
        for other in others:
            tell(relay.at[step], depth=other)

    def relayed(step, count):
        pl.semaphore_wait(relay.at[step], count)

    relay_on(0, along_y + along_x)

    @pl.when(jnp.logical_not(has_before))
    def _():
        field[0] = jnp.zeros(field.shape[1:], jnp.float32)

    @pl.when(jnp.logical_not(has_next))
    def _():
        field[planes + 1] = jnp.zeros(field.shape[1:], jnp.float32)

    @pl.when(jnp.logical_not(has_above))
    def _():
        top[...] = jnp.zeros(top.shape, jnp.float32)

    @pl.when(jnp.logical_not(has_below))
    def _():
        bottom[...] = jnp.zeros(bottom.shape, jnp.float32)

    _, material_count, knots = tf_color.shape
    for copy in small:
        copy.wait()
    lane = lax.broadcasted_iota(jnp.int32, (8, LANES), 1)
    sub = lax.broadcasted_iota(jnp.int32, (8, LANES), 0)

    def table(row_of):
        parts = [row_of(m) for m in range(material_count)]
        parts.append(jnp.zeros((1, LANES - material_count * knots), jnp.float32))
        base = jnp.broadcast_to(jnp.concatenate(parts, axis=1), (8, LANES))
        return base, pltpu.roll(base, LANES - 1, 1) - base

    tables = [table(lambda m, c=c: tf_color[c, pl.ds(m, 1), :]) for c in range(3)]
    tables.append(table(lambda m: tf_opacity[pl.ds(m, 1), :]))

    along_lanes = lax.GatherDimensionNumbers(
        offset_dims=(),
        collapsed_slice_dims=(1,),
        start_index_map=(1,),
        operand_batching_dims=(0,),
        start_indices_batching_dims=(0,),
    )

    def look(entry, index):
        return lax.gather(
            entry,
            index[:, :, None],
            along_lanes,
            slice_sizes=(1, 1),
            mode=lax.GatherScatterMode.PROMISE_IN_BOUNDS,
        )

    cells = [(z, half) for half in range(rows // 8) for z in range(planes)]

    def look_up_tile(t, slot):
        at = pl.multiple_of(t * LANES, LANES)
        for n, (z, half) in enumerate(cells):
            band = pl.ds(8 * half, 8)
            sample = field[z + 1, band, pl.ds(at + LANES, LANES)]
            position = jnp.clip((sample + 3.0) * ((knots - 1) / 6.0), 0.0, knots - 1.0)
            knot = position.astype(jnp.int32)
            part = position - knot.astype(jnp.float32)
            index = (mats[z, band, pl.ds(at, LANES)] * knots + knot) & (LANES - 1)
            for c, (base, step) in enumerate(tables):
                looked[slot, n, c] = look(base, index) + part * look(step, index)

    def weigh_tile(t, slot):
        at = pl.multiple_of(t * LANES, LANES)
        occupied = flags[0, 0, t].astype(jnp.float32)
        passed = None
        for n, (z, half) in enumerate(cells):
            band = pl.ds(8 * half, 8)
            kept = jnp.exp(-(looked[slot, n, 3] * occupied))
            weight = 1.0 - kept if z == 0 else passed * (1.0 - kept)
            for c in range(3):
                shade[c, z, band, pl.ds(at, LANES)] = looked[slot, n, c] * weight
            passed = kept if z == 0 else passed * kept
            if z == planes - 1:
                through[band, pl.ds(at, LANES)] = passed

    def look_up(i):
        for u in range(LOOK_UNROLL):
            look_up_tile(i * LOOK_UNROLL + u, u)

    def weigh(i):
        for u in range(LOOK_UNROLL):
            weigh_tile(i * LOOK_UNROLL + u, u)

    def loaded(j):
        for copy in load(j):
            copy.wait()

    steps = per_chunk // LOOK_UNROLL

    def weigh_and_look_up(i):
        weigh(i - 1)
        look_up(i)

    loaded(0)
    look_up(0)
    pl.loop(1, steps)(weigh_and_look_up)
    relayed(0, len(along_y + along_x))
    relay_on(1, across_x)

    @pl.loop(1, SIDE)
    def _(j):
        loaded(j)
        pl.loop(j * steps, (j + 1) * steps)(weigh_and_look_up)

    weigh(SIDE * steps - 1)

    pl.when(has_above)(lambda: row_copy(0).wait_recv())
    pl.when(has_below)(lambda: row_copy(1).wait_recv())

    def core_copy(j):
        mine = pl.ds(j * per_chunk, per_chunk)
        return pltpu.make_async_remote_copy(
            src_ref=packed.at[1 - core, mine],
            dst_ref=packed.at[2, mine],
            send_sem=core_send.at[j],
            recv_sem=core_recv.at[j],
            device_id={"depth": partner},
            device_id_type=MESH,
        )

    def piece_copy(k, source):
        return pltpu.make_async_remote_copy(
            src_ref=outgoing.at[k],
            dst_ref=pieces.at[source],
            send_sem=piece_send.at[k],
            recv_sem=piece_recv.at[source],
            device_id={"depth": 2 * k + core},
            device_id_type=MESH,
        )

    def light_tile(t):
        at = pl.multiple_of(t * LANES, LANES)

        def tile(z, half, shift=0):
            return field[z, pl.ds(8 * half, 8), pl.ds(at + LANES + shift * LANES, LANES)]

        sums = [[None] * 4 for _ in range(2)]
        for half in range(2):
            sums[half][3] = through[pl.ds(8 * half, 8), pl.ds(at, LANES)]
        column = [[tile(z, half) for half in range(2)] for z in range(planes + 2)]
        for z in range(planes):
            above = jnp.broadcast_to(top[z, :, pl.ds(at, LANES)], (8, LANES))
            below = jnp.broadcast_to(bottom[z, :, pl.ds(at, LANES)], (8, LANES))
            here = column[z + 1]
            for half in range(2):
                mid = here[half]
                left = pltpu.roll(jnp.where(lane == LANES - 1, tile(z + 1, half, -1), mid), 1, 1)
                right = pltpu.roll(jnp.where(lane == 0, tile(z + 1, half, 1), mid), LANES - 1, 1)
                up = pltpu.roll(jnp.where(sub == 7, above if half == 0 else here[0], mid), 1, 0)
                down = pltpu.roll(jnp.where(sub == 0, below if half == 1 else here[1], mid), 7, 0)
                gx = right - left
                gy = down - up
                gz = column[z + 2][half] - column[z][half]
                facing = gx + 2.0 * (gy + gz)
                steep = gx * gx + gy * gy + gz * gz
                light = 0.3 + (0.7 / 3.0) * jnp.abs(facing) * lax.rsqrt(4.0 + steep)
                for c in range(3):
                    term = shade[c, z, pl.ds(8 * half, 8), pl.ds(at, LANES)] * light
                    sums[half][c] = term if z == 0 else sums[half][c] + term
        return sums

    def pack(j):
        def pack_tile(y):
            sums = light_tile(owner(j) * per_chunk + y)
            for c in range(4):
                first, second = sums[0][c], sums[1][c]
                packed[0, j * per_chunk + y, c] = jnp.where(
                    lane < HALF, first, pltpu.roll(second, HALF, 1)
                )
                packed[1, j * per_chunk + y, c] = jnp.where(
                    lane < HALF, pltpu.roll(first, HALF, 1), second
                )

        @pl.loop(0, per_chunk // LIGHT_UNROLL)
        def _(i):
            for u in range(LIGHT_UNROLL):
                pack_tile(i * LIGHT_UNROLL + u)

    def over(near, far):
        return [near[c] + near[3] * far[c] for c in range(3)] + [near[3] * far[3]]

    def join(j):
        if j == 0:
            relayed(1, len(across_x))
        core_copy(j).wait_recv()
        for y in range(per_chunk):
            k = owner(j) * SIDE + y
            near = [packed[2 * core, j * per_chunk + y, c] for c in range(4)]
            far = [packed[2 - core, j * per_chunk + y, c] for c in range(4)]
            for c, value in enumerate(over(near, far)):
                outgoing[k, c] = value
        for y in range(per_chunk):
            k = owner(j) * SIDE + y
            pl.when(k != chip)(lambda k=k: piece_copy(k, chip).start())

    for j in range(SIDE):
        pl.when(has_before)(lambda: plane_copy(0, owner(j)).wait_recv())
        pl.when(has_next)(lambda: plane_copy(1, owner(j)).wait_recv())
        pack(j)
        core_copy(j).start()
        if j > 0:
            join(j - 1)
    join(SIDE - 1)

    pieces[chip] = outgoing[chip]

    pl.when(has_below)(lambda: row_copy(0).wait_send())
    pl.when(has_above)(lambda: row_copy(1).wait_send())
    for j in range(SIDE):
        pl.when(has_next)(lambda: plane_copy(0, wanted(0, j)).wait_send())
        pl.when(has_before)(lambda: plane_copy(1, wanted(1, j)).wait_send())
        core_copy(j).wait_send()

    @pl.loop(0, CHIPS)
    def _(k):
        pl.when(k != chip)(lambda: piece_copy(k, chip).wait_send())

    @pl.loop(0, CHIPS)
    def _(k):
        pl.when(k != chip)(lambda: piece_copy(k, k).wait_recv())

    held = [[pieces[k, c] for c in range(4)] for k in range(CHIPS)]
    while len(held) > 1:
        held = [over(near, far) for near, far in zip(held[0::2], held[1::2])]
    held = held[0]
    for c in range(4):
        value = held[c] if c < 3 else 1.0 - held[c]
        image[c, pl.ds(0, 8), :] = value[:, :HALF]
        image[c, pl.ds(8, 8), :] = pltpu.roll(value, HALF, 1)[:, :HALF]


def on_device(density, materials, occupancy_flags, tf_color, tf_opacity):
    planes, rows, columns = density.shape
    tiles = columns // LANES
    color = jnp.transpose(tf_color, (1, 0, 2))
    block = (4, 8, LANES)
    f32 = jnp.float32
    dma = pltpu.SemaphoreType.DMA
    return pl.pallas_call(
        kernel,
        out_shape=pltpu.VMEM((4, rows, columns // lax.axis_size("depth")), f32),
        in_specs=[
            pl.BlockSpec(memory_space=pltpu.HBM),
        ]
        * 5,
        out_specs=pl.BlockSpec(memory_space=pltpu.VMEM),
        scratch_shapes=[
            pltpu.VMEM((planes + 2, rows, columns + 2 * LANES), f32),
            pltpu.VMEM((planes, rows, columns), jnp.int32),
            pltpu.VMEM((planes, 1, columns), f32),
            pltpu.VMEM((planes, 1, columns), f32),
            pltpu.VMEM((3, planes, rows, columns), f32),
            pltpu.VMEM((rows, columns), f32),
            pltpu.VMEM((3, tiles) + block, f32),
            pltpu.VMEM((CHIPS,) + block, f32),
            pltpu.VMEM((CHIPS,) + block, f32),
            pltpu.VMEM((LOOK_UNROLL, 2 * planes, 4, 8, LANES), f32),
            pltpu.SMEM(occupancy_flags.shape, jnp.int32),
            pltpu.VMEM(color.shape, f32),
            pltpu.VMEM(tf_opacity.shape, f32),
            dma((3,)),
            pltpu.SemaphoreType.REGULAR((2,)),
            dma((2, SIDE)),
            dma((2, SIDE)),
            dma((2, SIDE)),
            dma((2,)),
            dma((2,)),
            dma((SIDE,)),
            dma((SIDE,)),
            dma((CHIPS,)),
            dma((CHIPS,)),
        ],
        compiler_params=pltpu.CompilerParams(
            collective_id=0, has_side_effects=True, vmem_limit_bytes=60 << 20
        ),
        name="render",
    )(density, materials, occupancy_flags, color, tf_opacity)


def solution(mesh):
    placed = (
        P("depth", "strip", None),
        P("depth", "strip", None),
        P("depth", "strip", None),
        P(),
        P(),
    )
    return jax.shard_map(
        on_device, mesh=mesh, in_specs=placed, out_specs=P(None, "strip", "depth"), check_vma=False
    )
```

```python
import jax
import jax.numpy as jnp
from jax import lax
from jax.experimental import pallas as pl
from jax.experimental.pallas import tpu as pltpu
from jax.sharding import PartitionSpec as P

MESH = pl.DeviceIdType.MESH
LANES = 128
HALF = LANES // 2
SIDE = 4
CHIPS = SIDE * SIDE
LOOK_UNROLL = 4
LIGHT_UNROLL = 2


def kernel(
    density, materials, flags_in, color_in, opacity_in, image,
    field, mats, top, bottom, shade, through, packed, outgoing, pieces,
    looked, flags, tf_color, tf_opacity, small_sem, relay,
    load_sem, plane_send, plane_recv, row_send, row_recv,
    core_send, core_recv, piece_send, piece_recv,
):
    depth_count = lax.axis_size("depth")
    strip_count = lax.axis_size("strip")
    d = lax.axis_index("depth")
    s = lax.axis_index("strip")
    core = lax.rem(d, 2)
    chip = d // 2
    chip_x = chip // SIDE
    partner = d + 1 - 2 * core
    cross = d - 1 + 2 * core
    cross_ok = jnp.logical_and(cross >= 0, cross < depth_count)
    planes, rows, columns = density.shape
    chunk = columns // SIDE
    tiles = columns // LANES
    per_chunk = chunk // LANES

    chip_y = lax.rem(chip, SIDE)

    def on_chip(x, y):
        return 2 * (lax.rem(x, SIDE) * SIDE + lax.rem(y, SIDE)) + core

    along_x = [on_chip(chip_x + step, chip_y) for step in (1, SIDE - 1)]
    across_x = along_x + [on_chip(chip_x + 2, chip_y)]
    along_y = [on_chip(chip_x, chip_y + step) for step in (1, SIDE - 1)]
    barrier = pltpu.get_barrier_semaphore()

    def tell(sem, **where):
        pl.semaphore_signal(sem, inc=1, device_id=where, device_id_type=MESH)

    pl.when(cross_ok)(lambda: tell(barrier, depth=cross))
    pl.when(s > 0)(lambda: tell(barrier, strip=s - 1))
    pl.when(s < strip_count - 1)(lambda: tell(barrier, strip=s + 1))
    tell(barrier, depth=partner)
    for other in along_x + along_y:
        tell(barrier, depth=other)

    def load(j):
        start = pl.multiple_of(j * chunk, LANES)
        cols = pl.ds(start, chunk)
        return (
            pltpu.make_async_copy(
                density.at[:, :, cols],
                field.at[pl.ds(1, planes), :, pl.ds(start + LANES, chunk)],
                load_sem.at[0, j],
            ),
            pltpu.make_async_copy(
                materials.at[:, :, cols], mats.at[:, :, cols], load_sem.at[1, j]
            ),
        )

    small = (
        pltpu.make_async_copy(flags_in, flags, small_sem.at[0]),
        pltpu.make_async_copy(color_in, tf_color, small_sem.at[1]),
        pltpu.make_async_copy(opacity_in, tf_opacity, small_sem.at[2]),
    )
    for copy in small:
        copy.start()
    for j in range(SIDE):
        for copy in load(j):
            copy.start()

    edge = jnp.zeros((planes, rows, LANES), jnp.float32)
    field[pl.ds(1, planes), :, pl.ds(0, LANES)] = edge
    field[pl.ds(1, planes), :, pl.ds(columns + LANES, LANES)] = edge

    expected = (
        1
        + len(along_x)
        + len(along_y)
        + cross_ok.astype(jnp.int32)
        + (s > 0).astype(jnp.int32)
        + (s < strip_count - 1).astype(jnp.int32)
    )
    pl.semaphore_wait(barrier, expected)

    def plane_copy(way, j):
        source = planes - 1 if way == 0 else 0
        target = 0 if way == 0 else planes + 1
        return pltpu.make_async_remote_copy(
            src_ref=density.at[source, :, pl.ds(j * chunk, chunk)],
            dst_ref=field.at[target, :, pl.ds(j * chunk + LANES, chunk)],
            send_sem=plane_send.at[way, j],
            recv_sem=plane_recv.at[way, j],
            device_id={"depth": d + 1 if way == 0 else d - 1},
            device_id_type=MESH,
        )

    def row_copy(way):
        source = rows - 1 if way == 0 else 0
        return pltpu.make_async_remote_copy(
            src_ref=density.at[:, pl.ds(source, 1), :],
            dst_ref=top if way == 0 else bottom,
            send_sem=row_send.at[way],
            recv_sem=row_recv.at[way],
            device_id={"strip": s + 1 if way == 0 else s - 1},
            device_id_type=MESH,
        )

    has_next = d < depth_count - 1
    has_before = d > 0
    has_below = s < strip_count - 1
    has_above = s > 0

    pl.when(has_below)(lambda: row_copy(0).start())
    pl.when(has_above)(lambda: row_copy(1).start())
    for j in range(SIDE):
        pl.when(has_next)(lambda: plane_copy(0, j).start())
        pl.when(has_before)(lambda: plane_copy(1, j).start())

    def relay_on(step, others):
        for other in others:
            tell(relay.at[step], depth=other)

    def relayed(step, count):
        pl.semaphore_wait(relay.at[step], count)

    relay_on(0, along_y + along_x)

    @pl.when(jnp.logical_not(has_before))
    def _():
        field[0] = jnp.zeros(field.shape[1:], jnp.float32)

    @pl.when(jnp.logical_not(has_next))
    def _():
        field[planes + 1] = jnp.zeros(field.shape[1:], jnp.float32)

    @pl.when(jnp.logical_not(has_above))
    def _():
        top[...] = jnp.zeros(top.shape, jnp.float32)

    @pl.when(jnp.logical_not(has_below))
    def _():
        bottom[...] = jnp.zeros(bottom.shape, jnp.float32)

    _, material_count, knots = tf_color.shape
    for copy in small:
        copy.wait()
    lane = lax.broadcasted_iota(jnp.int32, (8, LANES), 1)
    sub = lax.broadcasted_iota(jnp.int32, (8, LANES), 0)

    def table(row_of):
        parts = [row_of(m) for m in range(material_count)]
        parts.append(jnp.zeros((1, LANES - material_count * knots), jnp.float32))
        base = jnp.broadcast_to(jnp.concatenate(parts, axis=1), (8, LANES))
        return base, pltpu.roll(base, LANES - 1, 1) - base

    tables = [table(lambda m, c=c: tf_color[c, pl.ds(m, 1), :]) for c in range(3)]
    tables.append(table(lambda m: tf_opacity[pl.ds(m, 1), :]))

    along_lanes = lax.GatherDimensionNumbers(
        offset_dims=(),
        collapsed_slice_dims=(1,),
        start_index_map=(1,),
        operand_batching_dims=(0,),
        start_indices_batching_dims=(0,),
    )

    def look(entry, index):
        return lax.gather(
            entry,
            index[:, :, None],
            along_lanes,
            slice_sizes=(1, 1),
            mode=lax.GatherScatterMode.PROMISE_IN_BOUNDS,
        )

    cells = [(z, half) for half in range(rows // 8) for z in range(planes)]

    def look_up_tile(t, slot):
        at = pl.multiple_of(t * LANES, LANES)
        for n, (z, half) in enumerate(cells):
            band = pl.ds(8 * half, 8)
            sample = field[z + 1, band, pl.ds(at + LANES, LANES)]
            position = jnp.clip((sample + 3.0) * ((knots - 1) / 6.0), 0.0, knots - 1.0)
            knot = position.astype(jnp.int32)
            part = position - knot.astype(jnp.float32)
            index = (mats[z, band, pl.ds(at, LANES)] * knots + knot) & (LANES - 1)
            for c, (base, step) in enumerate(tables):
                looked[slot, n, c] = look(base, index) + part * look(step, index)

    def weigh_tile(t, slot):
        at = pl.multiple_of(t * LANES, LANES)
        occupied = flags[0, 0, t].astype(jnp.float32)
        passed = None
        for n, (z, half) in enumerate(cells):
            band = pl.ds(8 * half, 8)
            kept = jnp.exp(-(looked[slot, n, 3] * occupied))
            weight = 1.0 - kept if z == 0 else passed * (1.0 - kept)
            for c in range(3):
                shade[c, z, band, pl.ds(at, LANES)] = looked[slot, n, c] * weight
            passed = kept if z == 0 else passed * kept
            if z == planes - 1:
                through[band, pl.ds(at, LANES)] = passed

    def look_up(i):
        for u in range(LOOK_UNROLL):
            look_up_tile(i * LOOK_UNROLL + u, u)

    def weigh(i):
        for u in range(LOOK_UNROLL):
            weigh_tile(i * LOOK_UNROLL + u, u)

    def loaded(j):
        for copy in load(j):
            copy.wait()

    steps = per_chunk // LOOK_UNROLL

    def weigh_and_look_up(i):
        weigh(i - 1)
        look_up(i)

    loaded(0)
    look_up(0)
    pl.loop(1, steps)(weigh_and_look_up)
    relayed(0, len(along_y + along_x))
    relay_on(1, across_x)

    @pl.loop(1, SIDE)
    def _(j):
        loaded(j)
        pl.loop(j * steps, (j + 1) * steps)(weigh_and_look_up)

    weigh(SIDE * steps - 1)

    pl.when(has_above)(lambda: row_copy(0).wait_recv())
    pl.when(has_below)(lambda: row_copy(1).wait_recv())

    def core_copy(j):
        mine = pl.ds(j * per_chunk, per_chunk)
        return pltpu.make_async_remote_copy(
            src_ref=packed.at[1 - core, mine],
            dst_ref=packed.at[2, mine],
            send_sem=core_send.at[j],
            recv_sem=core_recv.at[j],
            device_id={"depth": partner},
            device_id_type=MESH,
        )

    def piece_copy(k, source):
        return pltpu.make_async_remote_copy(
            src_ref=outgoing.at[k],
            dst_ref=pieces.at[source],
            send_sem=piece_send.at[k],
            recv_sem=piece_recv.at[source],
            device_id={"depth": 2 * k + core},
            device_id_type=MESH,
        )

    def light_tile(t):
        at = pl.multiple_of(t * LANES, LANES)

        def tile(z, half, shift=0):
            return field[z, pl.ds(8 * half, 8), pl.ds(at + LANES + shift * LANES, LANES)]

        sums = [[None] * 4 for _ in range(2)]
        for half in range(2):
            sums[half][3] = through[pl.ds(8 * half, 8), pl.ds(at, LANES)]
        column = [[tile(z, half) for half in range(2)] for z in range(planes + 2)]
        for z in range(planes):
            above = jnp.broadcast_to(top[z, :, pl.ds(at, LANES)], (8, LANES))
            below = jnp.broadcast_to(bottom[z, :, pl.ds(at, LANES)], (8, LANES))
            here = column[z + 1]
            for half in range(2):
                mid = here[half]
                left = pltpu.roll(jnp.where(lane == LANES - 1, tile(z + 1, half, -1), mid), 1, 1)
                right = pltpu.roll(jnp.where(lane == 0, tile(z + 1, half, 1), mid), LANES - 1, 1)
                up = pltpu.roll(jnp.where(sub == 7, above if half == 0 else here[0], mid), 1, 0)
                down = pltpu.roll(jnp.where(sub == 0, below if half == 1 else here[1], mid), 7, 0)
                gx = right - left
                gy = down - up
                gz = column[z + 2][half] - column[z][half]
                facing = gx + 2.0 * (gy + gz)
                steep = gx * gx + gy * gy + gz * gz
                light = 0.3 + (0.7 / 3.0) * jnp.abs(facing) * lax.rsqrt(4.0 + steep)
                for c in range(3):
                    term = shade[c, z, pl.ds(8 * half, 8), pl.ds(at, LANES)] * light
                    sums[half][c] = term if z == 0 else sums[half][c] + term
        return sums

    def pack(j):
        def pack_tile(y):
            sums = light_tile(j * per_chunk + y)
            for c in range(4):
                first, second = sums[0][c], sums[1][c]
                packed[0, j * per_chunk + y, c] = jnp.where(
                    lane < HALF, first, pltpu.roll(second, HALF, 1)
                )
                packed[1, j * per_chunk + y, c] = jnp.where(
                    lane < HALF, pltpu.roll(first, HALF, 1), second
                )

        @pl.loop(0, per_chunk // LIGHT_UNROLL)
        def _(i):
            for u in range(LIGHT_UNROLL):
                pack_tile(i * LIGHT_UNROLL + u)

    def over(near, far):
        return [near[c] + near[3] * far[c] for c in range(3)] + [near[3] * far[3]]

    def join(j):
        if j == 0:
            relayed(1, len(across_x))
        core_copy(j).wait_recv()
        for y in range(per_chunk):
            k = j * per_chunk + y
            near = [packed[2 * core, j * per_chunk + y, c] for c in range(4)]
            far = [packed[2 - core, j * per_chunk + y, c] for c in range(4)]
            for c, value in enumerate(over(near, far)):
                outgoing[k, c] = value
        for y in range(per_chunk):
            k = j * per_chunk + y
            pl.when(k != chip)(lambda k=k: piece_copy(k, chip).start())

    for j in range(SIDE):
        pl.when(has_before)(lambda: plane_copy(0, j).wait_recv())
        pl.when(has_next)(lambda: plane_copy(1, j).wait_recv())
        pack(j)
        core_copy(j).start()
        if j > 0:
            join(j - 1)
    join(SIDE - 1)

    pieces[chip] = outgoing[chip]

    pl.when(has_below)(lambda: row_copy(0).wait_send())
    pl.when(has_above)(lambda: row_copy(1).wait_send())
    for j in range(SIDE):
        pl.when(has_next)(lambda: plane_copy(0, j).wait_send())
        pl.when(has_before)(lambda: plane_copy(1, j).wait_send())
        core_copy(j).wait_send()

    @pl.loop(0, CHIPS)
    def _(k):
        pl.when(k != chip)(lambda: piece_copy(k, chip).wait_send())

    @pl.loop(0, CHIPS)
    def _(k):
        pl.when(k != chip)(lambda: piece_copy(k, k).wait_recv())

    held = [[pieces[k, c] for c in range(4)] for k in range(CHIPS)]
    while len(held) > 1:
        held = [over(near, far) for near, far in zip(held[0::2], held[1::2])]
    held = held[0]
    for c in range(4):
        value = held[c] if c < 3 else 1.0 - held[c]
        image[c, pl.ds(0, 8), :] = value[:, :HALF]
        image[c, pl.ds(8, 8), :] = pltpu.roll(value, HALF, 1)[:, :HALF]


def on_device(density, materials, occupancy_flags, tf_color, tf_opacity):
    planes, rows, columns = density.shape
    tiles = columns // LANES
    color = jnp.transpose(tf_color, (1, 0, 2))
    block = (4, 8, LANES)
    f32 = jnp.float32
    dma = pltpu.SemaphoreType.DMA
    return pl.pallas_call(
        kernel,
        out_shape=pltpu.VMEM((4, rows, columns // lax.axis_size("depth")), f32),
        in_specs=[
            pl.BlockSpec(memory_space=pltpu.HBM),
        ]
        * 5,
        out_specs=pl.BlockSpec(memory_space=pltpu.VMEM),
        scratch_shapes=[
            pltpu.VMEM((planes + 2, rows, columns + 2 * LANES), f32),
            pltpu.VMEM((planes, rows, columns), jnp.int32),
            pltpu.VMEM((planes, 1, columns), f32),
            pltpu.VMEM((planes, 1, columns), f32),
            pltpu.VMEM((3, planes, rows, columns), f32),
            pltpu.VMEM((rows, columns), f32),
            pltpu.VMEM((3, tiles) + block, f32),
            pltpu.VMEM((CHIPS,) + block, f32),
            pltpu.VMEM((CHIPS,) + block, f32),
            pltpu.VMEM((LOOK_UNROLL, 2 * planes, 4, 8, LANES), f32),
            pltpu.SMEM(occupancy_flags.shape, jnp.int32),
            pltpu.VMEM(color.shape, f32),
            pltpu.VMEM(tf_opacity.shape, f32),
            dma((3,)),
            pltpu.SemaphoreType.REGULAR((2,)),
            dma((2, SIDE)),
            dma((2, SIDE)),
            dma((2, SIDE)),
            dma((2,)),
            dma((2,)),
            dma((SIDE,)),
            dma((SIDE,)),
            dma((CHIPS,)),
            dma((CHIPS,)),
        ],
        compiler_params=pltpu.CompilerParams(
            collective_id=0, has_side_effects=True, vmem_limit_bytes=60 << 20
        ),
        name="render",
    )(density, materials, occupancy_flags, color, tf_opacity)


def solution(mesh):
    placed = (
        P("depth", "strip", None),
        P("depth", "strip", None),
        P("depth", "strip", None),
        P(),
        P(),
    )
    return jax.shard_map(
        on_device, mesh=mesh, in_specs=placed, out_specs=P(None, "strip", "depth"), check_vma=False
    )
```

```python
import jax
import jax.numpy as jnp
from jax import lax
from jax.experimental import pallas as pl
from jax.experimental.pallas import tpu as pltpu
from jax.sharding import PartitionSpec as P

MESH = pl.DeviceIdType.MESH
LANES = 128
HALF = LANES // 2
SIDE = 4
CHIPS = SIDE * SIDE
LOOK_UNROLL = 4
LIGHT_UNROLL = 2


def kernel(
    density, materials, flags_in, color_in, opacity_in, image,
    field, mats, top, bottom, shade, through, packed, outgoing, pieces,
    looked, flags, tf_color, tf_opacity, small_sem, relay,
    load_sem, plane_send, plane_recv, row_send, row_recv,
    core_send, core_recv, piece_send, piece_recv,
):
    depth_count = lax.axis_size("depth")
    strip_count = lax.axis_size("strip")
    d = lax.axis_index("depth")
    s = lax.axis_index("strip")
    core = lax.rem(d, 2)
    chip = d // 2
    chip_x = chip // SIDE
    partner = d + 1 - 2 * core
    cross = d - 1 + 2 * core
    cross_ok = jnp.logical_and(cross >= 0, cross < depth_count)
    planes, rows, columns = density.shape
    chunk = columns // SIDE
    tiles = columns // LANES
    per_chunk = chunk // LANES

    chip_y = lax.rem(chip, SIDE)

    def on_chip(x, y):
        return 2 * (lax.rem(x, SIDE) * SIDE + lax.rem(y, SIDE)) + core

    along_x = [on_chip(chip_x + step, chip_y) for step in (1, SIDE - 1)]
    across_x = along_x + [on_chip(chip_x + 2, chip_y)]
    along_y = [on_chip(chip_x, chip_y + step) for step in (1, SIDE - 1)]
    barrier = pltpu.get_barrier_semaphore()

    def tell(sem, **where):
        pl.semaphore_signal(sem, inc=1, device_id=where, device_id_type=MESH)

    pl.when(cross_ok)(lambda: tell(barrier, depth=cross))
    pl.when(s > 0)(lambda: tell(barrier, strip=s - 1))
    pl.when(s < strip_count - 1)(lambda: tell(barrier, strip=s + 1))
    tell(barrier, depth=partner)
    for other in along_x + along_y:
        tell(barrier, depth=other)

    def load(j):
        start = pl.multiple_of(j * chunk, LANES)
        cols = pl.ds(start, chunk)
        return (
            pltpu.make_async_copy(
                density.at[:, :, cols],
                field.at[pl.ds(1, planes), :, pl.ds(start + LANES, chunk)],
                load_sem.at[0, j],
            ),
            pltpu.make_async_copy(
                materials.at[:, :, cols], mats.at[:, :, cols], load_sem.at[1, j]
            ),
        )

    small = (
        pltpu.make_async_copy(flags_in, flags, small_sem.at[0]),
        pltpu.make_async_copy(color_in, tf_color, small_sem.at[1]),
        pltpu.make_async_copy(opacity_in, tf_opacity, small_sem.at[2]),
    )
    for copy in small:
        copy.start()
    for j in range(SIDE):
        for copy in load(j):
            copy.start()

    edge = jnp.zeros((planes, rows, LANES), jnp.float32)
    field[pl.ds(1, planes), :, pl.ds(0, LANES)] = edge
    field[pl.ds(1, planes), :, pl.ds(columns + LANES, LANES)] = edge

    expected = (
        1
        + len(along_x)
        + len(along_y)
        + cross_ok.astype(jnp.int32)
        + (s > 0).astype(jnp.int32)
        + (s < strip_count - 1).astype(jnp.int32)
    )
    pl.semaphore_wait(barrier, expected)

    def plane_copy(way, j):
        source = planes - 1 if way == 0 else 0
        target = 0 if way == 0 else planes + 1
        return pltpu.make_async_remote_copy(
            src_ref=density.at[source, :, pl.ds(j * chunk, chunk)],
            dst_ref=field.at[target, :, pl.ds(j * chunk + LANES, chunk)],
            send_sem=plane_send.at[way, j],
            recv_sem=plane_recv.at[way, j],
            device_id={"depth": d + 1 if way == 0 else d - 1},
            device_id_type=MESH,
        )

    def row_copy(way):
        source = rows - 1 if way == 0 else 0
        return pltpu.make_async_remote_copy(
            src_ref=density.at[:, pl.ds(source, 1), :],
            dst_ref=top if way == 0 else bottom,
            send_sem=row_send.at[way],
            recv_sem=row_recv.at[way],
            device_id={"strip": s + 1 if way == 0 else s - 1},
            device_id_type=MESH,
        )

    has_next = d < depth_count - 1
    has_before = d > 0
    has_below = s < strip_count - 1
    has_above = s > 0

    for j in range(SIDE):
        pl.when(has_next)(lambda: plane_copy(0, j).start())
        pl.when(has_before)(lambda: plane_copy(1, j).start())
    pl.when(has_below)(lambda: row_copy(0).start())
    pl.when(has_above)(lambda: row_copy(1).start())

    def relay_on(step, others):
        for other in others:
            tell(relay.at[step], depth=other)

    def relayed(step, count):
        pl.semaphore_wait(relay.at[step], count)

    relay_on(0, along_y + along_x)

    @pl.when(jnp.logical_not(has_before))
    def _():
        field[0] = jnp.zeros(field.shape[1:], jnp.float32)

    @pl.when(jnp.logical_not(has_next))
    def _():
        field[planes + 1] = jnp.zeros(field.shape[1:], jnp.float32)

    @pl.when(jnp.logical_not(has_above))
    def _():
        top[...] = jnp.zeros(top.shape, jnp.float32)

    @pl.when(jnp.logical_not(has_below))
    def _():
        bottom[...] = jnp.zeros(bottom.shape, jnp.float32)

    _, material_count, knots = tf_color.shape
    for copy in small:
        copy.wait()
    lane = lax.broadcasted_iota(jnp.int32, (8, LANES), 1)
    sub = lax.broadcasted_iota(jnp.int32, (8, LANES), 0)

    def table(row_of):
        parts = [row_of(m) for m in range(material_count)]
        parts.append(jnp.zeros((1, LANES - material_count * knots), jnp.float32))
        base = jnp.broadcast_to(jnp.concatenate(parts, axis=1), (8, LANES))
        return base, pltpu.roll(base, LANES - 1, 1) - base

    tables = [table(lambda m, c=c: tf_color[c, pl.ds(m, 1), :]) for c in range(3)]
    tables.append(table(lambda m: tf_opacity[pl.ds(m, 1), :]))

    along_lanes = lax.GatherDimensionNumbers(
        offset_dims=(),
        collapsed_slice_dims=(1,),
        start_index_map=(1,),
        operand_batching_dims=(0,),
        start_indices_batching_dims=(0,),
    )

    def look(entry, index):
        return lax.gather(
            entry,
            index[:, :, None],
            along_lanes,
            slice_sizes=(1, 1),
            mode=lax.GatherScatterMode.PROMISE_IN_BOUNDS,
        )

    cells = [(z, half) for half in range(rows // 8) for z in range(planes)]

    def look_up_tile(t, slot):
        at = pl.multiple_of(t * LANES, LANES)
        for n, (z, half) in enumerate(cells):
            band = pl.ds(8 * half, 8)
            sample = field[z + 1, band, pl.ds(at + LANES, LANES)]
            position = jnp.clip((sample + 3.0) * ((knots - 1) / 6.0), 0.0, knots - 1.0)
            knot = position.astype(jnp.int32)
            part = position - knot.astype(jnp.float32)
            index = (mats[z, band, pl.ds(at, LANES)] * knots + knot) & (LANES - 1)
            for c, (base, step) in enumerate(tables):
                looked[slot, n, c] = look(base, index) + part * look(step, index)

    def weigh_tile(t, slot):
        at = pl.multiple_of(t * LANES, LANES)
        occupied = flags[0, 0, t].astype(jnp.float32)
        passed = None
        for n, (z, half) in enumerate(cells):
            band = pl.ds(8 * half, 8)
            kept = jnp.exp(-(looked[slot, n, 3] * occupied))
            weight = 1.0 - kept if z == 0 else passed * (1.0 - kept)
            for c in range(3):
                shade[c, z, band, pl.ds(at, LANES)] = looked[slot, n, c] * weight
            passed = kept if z == 0 else passed * kept
            if z == planes - 1:
                through[band, pl.ds(at, LANES)] = passed

    def look_up(i):
        for u in range(LOOK_UNROLL):
            look_up_tile(i * LOOK_UNROLL + u, u)

    def weigh(i):
        for u in range(LOOK_UNROLL):
            weigh_tile(i * LOOK_UNROLL + u, u)

    def loaded(j):
        for copy in load(j):
            copy.wait()

    steps = per_chunk // LOOK_UNROLL

    def weigh_and_look_up(i):
        weigh(i - 1)
        look_up(i)

    loaded(0)
    look_up(0)
    pl.loop(1, steps)(weigh_and_look_up)
    relayed(0, len(along_y + along_x))
    relay_on(1, across_x)

    @pl.loop(1, SIDE)
    def _(j):
        loaded(j)
        pl.loop(j * steps, (j + 1) * steps)(weigh_and_look_up)

    weigh(SIDE * steps - 1)

    pl.when(has_above)(lambda: row_copy(0).wait_recv())
    pl.when(has_below)(lambda: row_copy(1).wait_recv())

    def core_copy(j):
        mine = pl.ds(j * per_chunk, per_chunk)
        return pltpu.make_async_remote_copy(
            src_ref=packed.at[1 - core, mine],
            dst_ref=packed.at[2, mine],
            send_sem=core_send.at[j],
            recv_sem=core_recv.at[j],
            device_id={"depth": partner},
            device_id_type=MESH,
        )

    def piece_copy(k, source):
        return pltpu.make_async_remote_copy(
            src_ref=outgoing.at[k],
            dst_ref=pieces.at[source],
            send_sem=piece_send.at[k],
            recv_sem=piece_recv.at[source],
            device_id={"depth": 2 * k + core},
            device_id_type=MESH,
        )

    def light_tile(t):
        at = pl.multiple_of(t * LANES, LANES)

        def tile(z, half, shift=0):
            return field[z, pl.ds(8 * half, 8), pl.ds(at + LANES + shift * LANES, LANES)]

        sums = [[None] * 4 for _ in range(2)]
        for half in range(2):
            sums[half][3] = through[pl.ds(8 * half, 8), pl.ds(at, LANES)]
        column = [[tile(z, half) for half in range(2)] for z in range(planes + 2)]
        for z in range(planes):
            above = jnp.broadcast_to(top[z, :, pl.ds(at, LANES)], (8, LANES))
            below = jnp.broadcast_to(bottom[z, :, pl.ds(at, LANES)], (8, LANES))
            here = column[z + 1]
            for half in range(2):
                mid = here[half]
                left = pltpu.roll(jnp.where(lane == LANES - 1, tile(z + 1, half, -1), mid), 1, 1)
                right = pltpu.roll(jnp.where(lane == 0, tile(z + 1, half, 1), mid), LANES - 1, 1)
                up = pltpu.roll(jnp.where(sub == 7, above if half == 0 else here[0], mid), 1, 0)
                down = pltpu.roll(jnp.where(sub == 0, below if half == 1 else here[1], mid), 7, 0)
                gx = right - left
                gy = down - up
                gz = column[z + 2][half] - column[z][half]
                facing = gx + 2.0 * (gy + gz)
                steep = gx * gx + gy * gy + gz * gz
                light = 0.3 + (0.7 / 3.0) * jnp.abs(facing) * lax.rsqrt(4.0 + steep)
                for c in range(3):
                    term = shade[c, z, pl.ds(8 * half, 8), pl.ds(at, LANES)] * light
                    sums[half][c] = term if z == 0 else sums[half][c] + term
        return sums

    def pack(j):
        def pack_tile(y):
            sums = light_tile(j * per_chunk + y)
            for c in range(4):
                first, second = sums[0][c], sums[1][c]
                packed[0, j * per_chunk + y, c] = jnp.where(
                    lane < HALF, first, pltpu.roll(second, HALF, 1)
                )
                packed[1, j * per_chunk + y, c] = jnp.where(
                    lane < HALF, pltpu.roll(first, HALF, 1), second
                )

        @pl.loop(0, per_chunk // LIGHT_UNROLL)
        def _(i):
            for u in range(LIGHT_UNROLL):
                pack_tile(i * LIGHT_UNROLL + u)

    def over(near, far):
        return [near[c] + near[3] * far[c] for c in range(3)] + [near[3] * far[3]]

    def join(j):
        if j == 0:
            relayed(1, len(across_x))
        core_copy(j).wait_recv()
        for y in range(per_chunk):
            k = j * per_chunk + y
            near = [packed[2 * core, j * per_chunk + y, c] for c in range(4)]
            far = [packed[2 - core, j * per_chunk + y, c] for c in range(4)]
            for c, value in enumerate(over(near, far)):
                outgoing[k, c] = value
        for y in range(per_chunk):
            k = j * per_chunk + y
            pl.when(k != chip)(lambda k=k: piece_copy(k, chip).start())

    for j in range(SIDE):
        pl.when(has_before)(lambda: plane_copy(0, j).wait_recv())
        pl.when(has_next)(lambda: plane_copy(1, j).wait_recv())
        pack(j)
        core_copy(j).start()
        if j > 0:
            join(j - 1)
    join(SIDE - 1)

    pieces[chip] = outgoing[chip]

    pl.when(has_below)(lambda: row_copy(0).wait_send())
    pl.when(has_above)(lambda: row_copy(1).wait_send())
    for j in range(SIDE):
        pl.when(has_next)(lambda: plane_copy(0, j).wait_send())
        pl.when(has_before)(lambda: plane_copy(1, j).wait_send())
        core_copy(j).wait_send()

    @pl.loop(0, CHIPS)
    def _(k):
        pl.when(k != chip)(lambda: piece_copy(k, chip).wait_send())

    @pl.loop(0, CHIPS)
    def _(k):
        pl.when(k != chip)(lambda: piece_copy(k, k).wait_recv())

    held = [[pieces[k, c] for c in range(4)] for k in range(CHIPS)]
    while len(held) > 1:
        held = [over(near, far) for near, far in zip(held[0::2], held[1::2])]
    held = held[0]
    for c in range(4):
        value = held[c] if c < 3 else 1.0 - held[c]
        image[c, pl.ds(0, 8), :] = value[:, :HALF]
        image[c, pl.ds(8, 8), :] = pltpu.roll(value, HALF, 1)[:, :HALF]


def on_device(density, materials, occupancy_flags, tf_color, tf_opacity):
    planes, rows, columns = density.shape
    tiles = columns // LANES
    color = jnp.transpose(tf_color, (1, 0, 2))
    block = (4, 8, LANES)
    f32 = jnp.float32
    dma = pltpu.SemaphoreType.DMA
    return pl.pallas_call(
        kernel,
        out_shape=pltpu.VMEM((4, rows, columns // lax.axis_size("depth")), f32),
        in_specs=[
            pl.BlockSpec(memory_space=pltpu.HBM),
        ]
        * 5,
        out_specs=pl.BlockSpec(memory_space=pltpu.VMEM),
        scratch_shapes=[
            pltpu.VMEM((planes + 2, rows, columns + 2 * LANES), f32),
            pltpu.VMEM((planes, rows, columns), jnp.int32),
            pltpu.VMEM((planes, 1, columns), f32),
            pltpu.VMEM((planes, 1, columns), f32),
            pltpu.VMEM((3, planes, rows, columns), f32),
            pltpu.VMEM((rows, columns), f32),
            pltpu.VMEM((3, tiles) + block, f32),
            pltpu.VMEM((CHIPS,) + block, f32),
            pltpu.VMEM((CHIPS,) + block, f32),
            pltpu.VMEM((LOOK_UNROLL, 2 * planes, 4, 8, LANES), f32),
            pltpu.SMEM(occupancy_flags.shape, jnp.int32),
            pltpu.VMEM(color.shape, f32),
            pltpu.VMEM(tf_opacity.shape, f32),
            dma((3,)),
            pltpu.SemaphoreType.REGULAR((2,)),
            dma((2, SIDE)),
            dma((2, SIDE)),
            dma((2, SIDE)),
            dma((2,)),
            dma((2,)),
            dma((SIDE,)),
            dma((SIDE,)),
            dma((CHIPS,)),
            dma((CHIPS,)),
        ],
        compiler_params=pltpu.CompilerParams(
            collective_id=0, has_side_effects=True, vmem_limit_bytes=60 << 20
        ),
        name="render",
    )(density, materials, occupancy_flags, color, tf_opacity)


def solution(mesh):
    placed = (
        P("depth", "strip", None),
        P("depth", "strip", None),
        P("depth", "strip", None),
        P(),
        P(),
    )
    return jax.shard_map(
        on_device, mesh=mesh, in_specs=placed, out_specs=P(None, "strip", "depth"), check_vma=False
    )
```

```python
import jax
import jax.numpy as jnp
from jax import lax
from jax.experimental import pallas as pl
from jax.experimental.pallas import tpu as pltpu
from jax.sharding import PartitionSpec as P

MESH = pl.DeviceIdType.MESH
LANES = 128
HALF = LANES // 2
SIDE = 4
CHIPS = SIDE * SIDE
LOOK_UNROLL = 4
LIGHT_UNROLL = 2


def kernel(
    density, materials, flags_in, color_in, opacity_in, image,
    field, mats, top, bottom, shade, through, packed, outgoing, pieces,
    looked, flags, tf_color, tf_opacity, small_sem, relay,
    load_sem, plane_send, plane_recv, row_send, row_recv,
    core_send, core_recv, piece_send, piece_recv,
):
    depth_count = lax.axis_size("depth")
    strip_count = lax.axis_size("strip")
    d = lax.axis_index("depth")
    s = lax.axis_index("strip")
    core = lax.rem(d, 2)
    chip = d // 2
    chip_x = chip // SIDE
    partner = d + 1 - 2 * core
    cross = d - 1 + 2 * core
    cross_ok = jnp.logical_and(cross >= 0, cross < depth_count)
    planes, rows, columns = density.shape
    chunk = columns // SIDE
    tiles = columns // LANES
    per_chunk = chunk // LANES

    chip_y = lax.rem(chip, SIDE)

    def on_chip(x, y):
        return 2 * (lax.rem(x, SIDE) * SIDE + lax.rem(y, SIDE)) + core

    along_x = [on_chip(chip_x + step, chip_y) for step in (1, SIDE - 1)]
    across_x = along_x + [on_chip(chip_x + 2, chip_y)]
    along_y = [on_chip(chip_x, chip_y + step) for step in (1, SIDE - 1)]
    barrier = pltpu.get_barrier_semaphore()

    def tell(sem, **where):
        pl.semaphore_signal(sem, inc=1, device_id=where, device_id_type=MESH)

    for other in along_x + along_y:
        tell(barrier, depth=other)
    pl.when(cross_ok)(lambda: tell(barrier, depth=cross))
    pl.when(s > 0)(lambda: tell(barrier, strip=s - 1))
    pl.when(s < strip_count - 1)(lambda: tell(barrier, strip=s + 1))
    tell(barrier, depth=partner)

    def load(j):
        start = pl.multiple_of(j * chunk, LANES)
        cols = pl.ds(start, chunk)
        return (
            pltpu.make_async_copy(
                density.at[:, :, cols],
                field.at[pl.ds(1, planes), :, pl.ds(start + LANES, chunk)],
                load_sem.at[0, j],
            ),
            pltpu.make_async_copy(
                materials.at[:, :, cols], mats.at[:, :, cols], load_sem.at[1, j]
            ),
        )

    small = (
        pltpu.make_async_copy(flags_in, flags, small_sem.at[0]),
        pltpu.make_async_copy(color_in, tf_color, small_sem.at[1]),
        pltpu.make_async_copy(opacity_in, tf_opacity, small_sem.at[2]),
    )
    for copy in small:
        copy.start()
    for j in range(SIDE):
        for copy in load(j):
            copy.start()

    edge = jnp.zeros((planes, rows, LANES), jnp.float32)
    field[pl.ds(1, planes), :, pl.ds(0, LANES)] = edge
    field[pl.ds(1, planes), :, pl.ds(columns + LANES, LANES)] = edge

    expected = (
        1
        + len(along_x)
        + len(along_y)
        + cross_ok.astype(jnp.int32)
        + (s > 0).astype(jnp.int32)
        + (s < strip_count - 1).astype(jnp.int32)
    )
    pl.semaphore_wait(barrier, expected)

    def plane_copy(way, j):
        source = planes - 1 if way == 0 else 0
        target = 0 if way == 0 else planes + 1
        return pltpu.make_async_remote_copy(
            src_ref=density.at[source, :, pl.ds(j * chunk, chunk)],
            dst_ref=field.at[target, :, pl.ds(j * chunk + LANES, chunk)],
            send_sem=plane_send.at[way, j],
            recv_sem=plane_recv.at[way, j],
            device_id={"depth": d + 1 if way == 0 else d - 1},
            device_id_type=MESH,
        )

    def row_copy(way):
        source = rows - 1 if way == 0 else 0
        return pltpu.make_async_remote_copy(
            src_ref=density.at[:, pl.ds(source, 1), :],
            dst_ref=top if way == 0 else bottom,
            send_sem=row_send.at[way],
            recv_sem=row_recv.at[way],
            device_id={"strip": s + 1 if way == 0 else s - 1},
            device_id_type=MESH,
        )

    has_next = d < depth_count - 1
    has_before = d > 0
    has_below = s < strip_count - 1
    has_above = s > 0

    for j in range(SIDE):
        pl.when(has_next)(lambda: plane_copy(0, j).start())
        pl.when(has_before)(lambda: plane_copy(1, j).start())
    pl.when(has_below)(lambda: row_copy(0).start())
    pl.when(has_above)(lambda: row_copy(1).start())

    def relay_on(step, others):
        for other in others:
            tell(relay.at[step], depth=other)

    def relayed(step, count):
        pl.semaphore_wait(relay.at[step], count)

    relay_on(0, along_y + along_x)

    @pl.when(jnp.logical_not(has_before))
    def _():
        field[0] = jnp.zeros(field.shape[1:], jnp.float32)

    @pl.when(jnp.logical_not(has_next))
    def _():
        field[planes + 1] = jnp.zeros(field.shape[1:], jnp.float32)

    @pl.when(jnp.logical_not(has_above))
    def _():
        top[...] = jnp.zeros(top.shape, jnp.float32)

    @pl.when(jnp.logical_not(has_below))
    def _():
        bottom[...] = jnp.zeros(bottom.shape, jnp.float32)

    _, material_count, knots = tf_color.shape
    for copy in small:
        copy.wait()
    lane = lax.broadcasted_iota(jnp.int32, (8, LANES), 1)
    sub = lax.broadcasted_iota(jnp.int32, (8, LANES), 0)

    def table(row_of):
        parts = [row_of(m) for m in range(material_count)]
        parts.append(jnp.zeros((1, LANES - material_count * knots), jnp.float32))
        base = jnp.broadcast_to(jnp.concatenate(parts, axis=1), (8, LANES))
        return base, pltpu.roll(base, LANES - 1, 1) - base

    tables = [table(lambda m, c=c: tf_color[c, pl.ds(m, 1), :]) for c in range(3)]
    tables.append(table(lambda m: tf_opacity[pl.ds(m, 1), :]))

    along_lanes = lax.GatherDimensionNumbers(
        offset_dims=(),
        collapsed_slice_dims=(1,),
        start_index_map=(1,),
        operand_batching_dims=(0,),
        start_indices_batching_dims=(0,),
    )

    def look(entry, index):
        return lax.gather(
            entry,
            index[:, :, None],
            along_lanes,
            slice_sizes=(1, 1),
            mode=lax.GatherScatterMode.PROMISE_IN_BOUNDS,
        )

    cells = [(z, half) for half in range(rows // 8) for z in range(planes)]

    def look_up_tile(t, slot):
        at = pl.multiple_of(t * LANES, LANES)
        for n, (z, half) in enumerate(cells):
            band = pl.ds(8 * half, 8)
            sample = field[z + 1, band, pl.ds(at + LANES, LANES)]
            position = jnp.clip((sample + 3.0) * ((knots - 1) / 6.0), 0.0, knots - 1.0)
            knot = position.astype(jnp.int32)
            part = position - knot.astype(jnp.float32)
            index = (mats[z, band, pl.ds(at, LANES)] * knots + knot) & (LANES - 1)
            for c, (base, step) in enumerate(tables):
                looked[slot, n, c] = look(base, index) + part * look(step, index)

    def weigh_tile(t, slot):
        at = pl.multiple_of(t * LANES, LANES)
        occupied = flags[0, 0, t].astype(jnp.float32)
        passed = None
        for n, (z, half) in enumerate(cells):
            band = pl.ds(8 * half, 8)
            kept = jnp.exp(-(looked[slot, n, 3] * occupied))
            weight = 1.0 - kept if z == 0 else passed * (1.0 - kept)
            for c in range(3):
                shade[c, z, band, pl.ds(at, LANES)] = looked[slot, n, c] * weight
            passed = kept if z == 0 else passed * kept
            if z == planes - 1:
                through[band, pl.ds(at, LANES)] = passed

    def look_up(i):
        for u in range(LOOK_UNROLL):
            look_up_tile(i * LOOK_UNROLL + u, u)

    def weigh(i):
        for u in range(LOOK_UNROLL):
            weigh_tile(i * LOOK_UNROLL + u, u)

    def loaded(j):
        for copy in load(j):
            copy.wait()

    steps = per_chunk // LOOK_UNROLL

    def weigh_and_look_up(i):
        weigh(i - 1)
        look_up(i)

    loaded(0)
    look_up(0)
    pl.loop(1, steps)(weigh_and_look_up)
    relayed(0, len(along_y + along_x))
    relay_on(1, across_x)

    @pl.loop(1, SIDE)
    def _(j):
        loaded(j)
        pl.loop(j * steps, (j + 1) * steps)(weigh_and_look_up)

    weigh(SIDE * steps - 1)

    pl.when(has_above)(lambda: row_copy(0).wait_recv())
    pl.when(has_below)(lambda: row_copy(1).wait_recv())

    def core_copy(j):
        mine = pl.ds(j * per_chunk, per_chunk)
        return pltpu.make_async_remote_copy(
            src_ref=packed.at[1 - core, mine],
            dst_ref=packed.at[2, mine],
            send_sem=core_send.at[j],
            recv_sem=core_recv.at[j],
            device_id={"depth": partner},
            device_id_type=MESH,
        )

    def piece_copy(k, source):
        return pltpu.make_async_remote_copy(
            src_ref=outgoing.at[k],
            dst_ref=pieces.at[source],
            send_sem=piece_send.at[k],
            recv_sem=piece_recv.at[source],
            device_id={"depth": 2 * k + core},
            device_id_type=MESH,
        )

    def light_tile(t):
        at = pl.multiple_of(t * LANES, LANES)

        def tile(z, half, shift=0):
            return field[z, pl.ds(8 * half, 8), pl.ds(at + LANES + shift * LANES, LANES)]

        sums = [[None] * 4 for _ in range(2)]
        for half in range(2):
            sums[half][3] = through[pl.ds(8 * half, 8), pl.ds(at, LANES)]
        column = [[tile(z, half) for half in range(2)] for z in range(planes + 2)]
        for z in range(planes):
            above = jnp.broadcast_to(top[z, :, pl.ds(at, LANES)], (8, LANES))
            below = jnp.broadcast_to(bottom[z, :, pl.ds(at, LANES)], (8, LANES))
            here = column[z + 1]
            for half in range(2):
                mid = here[half]
                left = pltpu.roll(jnp.where(lane == LANES - 1, tile(z + 1, half, -1), mid), 1, 1)
                right = pltpu.roll(jnp.where(lane == 0, tile(z + 1, half, 1), mid), LANES - 1, 1)
                up = pltpu.roll(jnp.where(sub == 7, above if half == 0 else here[0], mid), 1, 0)
                down = pltpu.roll(jnp.where(sub == 0, below if half == 1 else here[1], mid), 7, 0)
                gx = right - left
                gy = down - up
                gz = column[z + 2][half] - column[z][half]
                facing = gx + 2.0 * (gy + gz)
                steep = gx * gx + gy * gy + gz * gz
                light = 0.3 + (0.7 / 3.0) * jnp.abs(facing) * lax.rsqrt(4.0 + steep)
                for c in range(3):
                    term = shade[c, z, pl.ds(8 * half, 8), pl.ds(at, LANES)] * light
                    sums[half][c] = term if z == 0 else sums[half][c] + term
        return sums

    def pack(j):
        def pack_tile(y):
            sums = light_tile(j * per_chunk + y)
            for c in range(4):
                first, second = sums[0][c], sums[1][c]
                packed[0, j * per_chunk + y, c] = jnp.where(
                    lane < HALF, first, pltpu.roll(second, HALF, 1)
                )
                packed[1, j * per_chunk + y, c] = jnp.where(
                    lane < HALF, pltpu.roll(first, HALF, 1), second
                )

        @pl.loop(0, per_chunk // LIGHT_UNROLL)
        def _(i):
            for u in range(LIGHT_UNROLL):
                pack_tile(i * LIGHT_UNROLL + u)

    def over(near, far):
        return [near[c] + near[3] * far[c] for c in range(3)] + [near[3] * far[3]]

    def join(j):
        if j == 0:
            relayed(1, len(across_x))
        core_copy(j).wait_recv()
        for y in range(per_chunk):
            k = j * per_chunk + y
            near = [packed[2 * core, j * per_chunk + y, c] for c in range(4)]
            far = [packed[2 - core, j * per_chunk + y, c] for c in range(4)]
            for c, value in enumerate(over(near, far)):
                outgoing[k, c] = value
        for y in range(per_chunk):
            k = j * per_chunk + y
            pl.when(k != chip)(lambda k=k: piece_copy(k, chip).start())

    for j in range(SIDE):
        pl.when(has_before)(lambda: plane_copy(0, j).wait_recv())
        pl.when(has_next)(lambda: plane_copy(1, j).wait_recv())
        pack(j)
        core_copy(j).start()
        if j > 0:
            join(j - 1)
    join(SIDE - 1)

    pieces[chip] = outgoing[chip]

    pl.when(has_below)(lambda: row_copy(0).wait_send())
    pl.when(has_above)(lambda: row_copy(1).wait_send())
    for j in range(SIDE):
        pl.when(has_next)(lambda: plane_copy(0, j).wait_send())
        pl.when(has_before)(lambda: plane_copy(1, j).wait_send())
        core_copy(j).wait_send()

    @pl.loop(0, CHIPS)
    def _(k):
        pl.when(k != chip)(lambda: piece_copy(k, chip).wait_send())

    @pl.loop(0, CHIPS)
    def _(k):
        pl.when(k != chip)(lambda: piece_copy(k, k).wait_recv())

    held = [[pieces[k, c] for c in range(4)] for k in range(CHIPS)]
    while len(held) > 1:
        held = [over(near, far) for near, far in zip(held[0::2], held[1::2])]
    held = held[0]
    for c in range(4):
        value = held[c] if c < 3 else 1.0 - held[c]
        image[c, pl.ds(0, 8), :] = value[:, :HALF]
        image[c, pl.ds(8, 8), :] = pltpu.roll(value, HALF, 1)[:, :HALF]


def on_device(density, materials, occupancy_flags, tf_color, tf_opacity):
    planes, rows, columns = density.shape
    tiles = columns // LANES
    color = jnp.transpose(tf_color, (1, 0, 2))
    block = (4, 8, LANES)
    f32 = jnp.float32
    dma = pltpu.SemaphoreType.DMA
    return pl.pallas_call(
        kernel,
        out_shape=pltpu.VMEM((4, rows, columns // lax.axis_size("depth")), f32),
        in_specs=[
            pl.BlockSpec(memory_space=pltpu.HBM),
        ]
        * 5,
        out_specs=pl.BlockSpec(memory_space=pltpu.VMEM),
        scratch_shapes=[
            pltpu.VMEM((planes + 2, rows, columns + 2 * LANES), f32),
            pltpu.VMEM((planes, rows, columns), jnp.int32),
            pltpu.VMEM((planes, 1, columns), f32),
            pltpu.VMEM((planes, 1, columns), f32),
            pltpu.VMEM((3, planes, rows, columns), f32),
            pltpu.VMEM((rows, columns), f32),
            pltpu.VMEM((3, tiles) + block, f32),
            pltpu.VMEM((CHIPS,) + block, f32),
            pltpu.VMEM((CHIPS,) + block, f32),
            pltpu.VMEM((LOOK_UNROLL, 2 * planes, 4, 8, LANES), f32),
            pltpu.SMEM(occupancy_flags.shape, jnp.int32),
            pltpu.VMEM(color.shape, f32),
            pltpu.VMEM(tf_opacity.shape, f32),
            dma((3,)),
            pltpu.SemaphoreType.REGULAR((2,)),
            dma((2, SIDE)),
            dma((2, SIDE)),
            dma((2, SIDE)),
            dma((2,)),
            dma((2,)),
            dma((SIDE,)),
            dma((SIDE,)),
            dma((CHIPS,)),
            dma((CHIPS,)),
        ],
        compiler_params=pltpu.CompilerParams(
            collective_id=0, has_side_effects=True, vmem_limit_bytes=60 << 20
        ),
        name="render",
    )(density, materials, occupancy_flags, color, tf_opacity)


def solution(mesh):
    placed = (
        P("depth", "strip", None),
        P("depth", "strip", None),
        P("depth", "strip", None),
        P(),
        P(),
    )
    return jax.shard_map(
        on_device, mesh=mesh, in_specs=placed, out_specs=P(None, "strip", "depth"), check_vma=False
    )
```
